32 devices in a mesh: shard: 8 (over y, x, core), seq: 4 (over z).
Axes of the slice: x: 2, y: 2, z: 4, core: 2. Of those that a mesh axis runs over, the one named last changes fastest.
Arguments:
- inputs: bfloat16 [16, 1376, 1024], P('shard', 'seq'), may hold values from -6 to 6
- teacher: bfloat16 [16, 1376, 1024], P('shard', 'seq'), may hold values from -20 to 20
- cotangent: bfloat16 [16, 1376, 1024], P('shard', 'seq'), may hold values from -6 to 6
- token_valid: int32 [16, 1376], P('shard'), may hold values from 0 to 1, as said below
- image_real: int32 [16], P('shard'), may hold values from 0 to 1, as said below
- w_qkv: bfloat16 [1024, 3072], P('shard'), may hold values from -0.1875 to 0.1875
- q_bias: bfloat16 [1024], P('shard'), may hold values from -3 to 3
- v_bias: bfloat16 [1024], P('shard'), may hold values from -3 to 3
- w_out: bfloat16 [1024, 1024], P('shard'), may hold values from -0.75 to 0.75
- out_bias: bfloat16 [1024], P('shard'), may hold values from -2 to 2
- norm1_gain: bfloat16 [1024], P('shard'), may hold values from 0.5 to 1.5
- norm1_bias: bfloat16 [1024], P('shard'), may hold values from -1 to 1
- scale1: bfloat16 [1024], P('shard'), may hold values from 0.5 to 1.5
- norm2_gain: bfloat16 [1024], P('shard'), may hold values from 0.5 to 1.5
- norm2_bias: bfloat16 [1024], P('shard'), may hold values from -1 to 1
- w_up: bfloat16 [1024, 4096], P('shard'), may hold values from -0.1875 to 0.1875
- up_bias: bfloat16 [4096], P('shard'), may hold values from -3 to 3
- w_down: bfloat16 [4096, 1024], P('shard'), may hold values from -0.1875 to 0.1875
- down_bias: bfloat16 [1024], P('shard'), may hold values from -2 to 2
- scale2: bfloat16 [1024], P('shard'), may hold values from 0.5 to 1.5
Outputs:
- result: bfloat16 [16, 1376, 1024], P('shard', 'seq')
- loss: float32 [], replicated
- grad_inputs: float32 [16, 1376, 1024], P('shard', 'seq')
- grad_w_qkv: float32 [1024, 3072], P('shard')
- grad_q_bias: float32 [1024], P('shard')
- grad_v_bias: float32 [1024], P('shard')
- grad_w_out: float32 [1024, 1024], P('shard')
- grad_out_bias: float32 [1024], P('shard')
- grad_norm1_gain: float32 [1024], P('shard')
- grad_norm1_bias: float32 [1024], P('shard')
- grad_scale1: float32 [1024], P('shard')
- grad_norm2_gain: float32 [1024], P('shard')
- grad_norm2_bias: float32 [1024], P('shard')
- grad_w_up: float32 [1024, 4096], P('shard')
- grad_up_bias: float32 [4096], P('shard')
- grad_w_down: float32 [4096, 1024], P('shard')
- grad_down_bias: float32 [1024], P('shard')
- grad_scale2: float32 [1024], P('shard')
The draws below stay inside these ranges and needn't reach their ends.
Inputs may be any that keep to these rules, and one draw needn't show every extreme that they name: `token_valid`: each row holds ones first, then zeros, with at least 344 ones and at most 1370. `image_real`: exactly 11 entries are 1.
All inputs are finite; a program needn't handle non-finite values.
Results may differ from the reference program's by a relative error of at most 0.022.
Values may be sent and summed in bfloat16 or wider, within the bound.
No kernel may reach another device: no remote copies, remote signals or barrier semaphores. Data moves between devices by JAX's collectives and lax.ppermute only.
A program may use at most 192 MiB of HBM per device.

```python
import jax
import jax.numpy as jnp
from jax import lax

D = 1024
FF = 4096
HEADS = 16
HEAD_DIM = 64
LEN = 1376
SLOTS = 16


def draw_token_valid(key, part):
    lengths = jax.random.randint(key, (SLOTS, 1), LEN // 4, LEN - 5)
    positions = jnp.arange(LEN, dtype=jnp.int32)[None, :]
    return (positions < lengths).astype(jnp.int32)


def draw_image_real(key, part):
    ranking = jax.random.permutation(key, SLOTS)
    return (ranking < SLOTS * 47 // 64).astype(jnp.int32)


def draw_teacher(key, part):
    frac = jnp.arange(SLOTS, dtype=jnp.float32) / max(SLOTS - 1, 1)
    noise = jnp.clip(jax.random.normal(key, (SLOTS, LEN, D), jnp.float32), -6.0, 6.0)
    spread = 0.5 + 2.5 * frac
    return (noise * spread[:, None, None]).astype(jnp.bfloat16)


def shard_levels(own_key, dims, split, least, largest):
    level, own = 1.0, jax.random.fold_in(own_key, 6)
    for dim, parts in split:
        heights = jnp.exp(jax.random.uniform(jax.random.fold_in(own, dim), (parts,), jnp.float32, least / len(split), largest / len(split)))
        level = level * jnp.repeat(heights, dims[dim] // parts).reshape([-1 if axis == dim else 1 for axis in range(len(dims))])
    return level


def normal_values(own_key, extent, width, reach, pieces=(), kind=jnp.bfloat16):
    level = shard_levels(own_key, extent, pieces, -0.22, 0.18) if pieces else 1.0
    values = jax.random.normal(own_key, extent, jnp.float32) * width * level
    return jnp.minimum(jnp.maximum(values, -reach), reach).astype(kind)


def setup_inputs(seed: int = 0) -> dict:
    streams_of = jax.random.split(jax.random.key(seed), 21)
    inputs = normal_values(streams_of[0], (SLOTS, LEN, D), 1.0, 6.0, ((0, 8), (1, 4)))
    teacher = draw_teacher(jax.random.fold_in(streams_of[20], 71), 0)
    cotangent = normal_values(streams_of[2], (SLOTS, LEN, D), 1.0, 6.0, ((0, 8), (1, 4)))
    token_valid = draw_token_valid(jax.random.fold_in(streams_of[20], 71), 0)
    image_real = draw_image_real(jax.random.fold_in(streams_of[20], 71), 0)
    w_qkv = normal_values(streams_of[5], (D, 3 * D), D ** -0.5, 0.1875, ((0, 8),))
    q_bias = normal_values(streams_of[6], (D,), 0.5, 3.0, ((0, 8),))
    v_bias = normal_values(streams_of[7], (D,), 0.5, 3.0, ((0, 8),))
    w_out = normal_values(streams_of[8], (D, D), (D // 16) ** -0.5, 0.75, ((0, 8),))
    out_bias = normal_values(streams_of[9], (D,), 0.3, 2.0, ((0, 8),))
    norm1_gain = jnp.clip(1.0 + 0.1 * jax.random.normal(streams_of[10], (D,), jnp.float32), 0.5, 1.5).astype(jnp.bfloat16)
    norm1_bias = normal_values(streams_of[11], (D,), 0.2, 1.0, ((0, 8),))
    scale1 = jnp.clip(1.0 + 0.1 * jax.random.normal(streams_of[12], (D,), jnp.float32), 0.5, 1.5).astype(jnp.bfloat16)
    norm2_gain = jnp.clip(1.0 + 0.1 * jax.random.normal(streams_of[13], (D,), jnp.float32), 0.5, 1.5).astype(jnp.bfloat16)
    norm2_bias = normal_values(streams_of[14], (D,), 0.2, 1.0, ((0, 8),))
    w_up = normal_values(streams_of[15], (D, FF), D ** -0.5, 0.1875, ((0, 8),))
    up_bias = normal_values(streams_of[16], (FF,), 0.5, 3.0, ((0, 8),))
    w_down = normal_values(streams_of[17], (FF, D), (FF // 4) ** -0.5, 0.1875, ((0, 8),))
    down_bias = normal_values(streams_of[18], (D,), 0.3, 2.0, ((0, 8),))
    scale2 = jnp.clip(1.0 + 0.1 * jax.random.normal(streams_of[19], (D,), jnp.float32), 0.5, 1.5).astype(jnp.bfloat16)
    return {"inputs": inputs, "teacher": teacher, "cotangent": cotangent, "token_valid": token_valid, "image_real": image_real, "w_qkv": w_qkv, "q_bias": q_bias, "v_bias": v_bias, "w_out": w_out, "out_bias": out_bias, "norm1_gain": norm1_gain, "norm1_bias": norm1_bias, "scale1": scale1, "norm2_gain": norm2_gain, "norm2_bias": norm2_bias, "w_up": w_up, "up_bias": up_bias, "w_down": w_down, "down_bias": down_bias, "scale2": scale2}


@jax.custom_vjp
def low(v):
    return lax.optimization_barrier(v.astype(jnp.bfloat16)).astype(jnp.float32)

@jax.custom_vjp
def low_back(v):
    return v

def low_keep(v):
    return (low(v), None)

def low_pass(kept, grad):
    return (grad,)

def back_keep(v):
    return (v, None)

def back_low(kept, grad):
    return (low(grad),)
low.defvjp(low_keep, low_pass)
low_back.defvjp(back_keep, back_low)

def matmul_high(left, right):
    return jnp.dot(left, right, precision=lax.Precision.HIGHEST)

def layer_norm(values, gain, shift):
    center = values - lax.optimization_barrier(jnp.mean(values, axis=-1, keepdims=True))
    spread = lax.optimization_barrier(jnp.mean(center * center, axis=-1, keepdims=True))
    return center * lax.rsqrt(spread + 1e-06) * gain + shift

def attend_image(queries, key_rows, value_rows, key_live):
    query_heads = queries.reshape(LEN, HEADS, HEAD_DIM)
    key_heads = key_rows.reshape(LEN, HEADS, HEAD_DIM)
    value_heads = value_rows.reshape(LEN, HEADS, HEAD_DIM)
    scores = jnp.einsum('qhd,khd->hqk', query_heads, key_heads, precision=lax.Precision.HIGHEST) * HEAD_DIM ** (-0.5)
    scores = jnp.where(key_live[None, None, :] > 0, low_back(scores), -1000000000.0)
    attn_prob = low(jax.nn.softmax(scores, axis=-1))
    mixed_rows = jnp.einsum('hqk,khd->qhd', attn_prob, value_heads, precision=lax.Precision.HIGHEST)
    return mixed_rows.reshape(LEN, HEADS * HEAD_DIM)

def forward_image(params, image_in, teacher_img, live, count):
    qkv_mat, qbias_vec, vbias_vec, out_mat, obias_vec, gain_one, shift_one, layer_one, gain_two, shift_two, up_mat, ubias_vec, down_mat, dbias_vec, layer_two = params
    normed1 = low(layer_norm(image_in, gain_one, shift_one))
    qkv_out = matmul_high(normed1, qkv_mat)
    queries = low_back(low(qkv_out[:, 0:D] + qbias_vec))
    key_rows = low_back(low(qkv_out[:, D:2 * D]))
    value_rows = low_back(low(qkv_out[:, 2 * D:3 * D] + vbias_vec))
    mixed_rows = low_back(low(jax.checkpoint(attend_image)(queries, key_rows, value_rows, live)))
    attn_out = low_back(matmul_high(mixed_rows, out_mat) + obias_vec)
    resid_one = image_in + layer_one * attn_out
    normed2 = low(layer_norm(resid_one, gain_two, shift_two))
    hidden_pre = low_back(matmul_high(normed2, up_mat) + ubias_vec)
    hidden_act = low(jax.nn.gelu(hidden_pre, approximate=False))
    branch_out = low_back(matmul_high(hidden_act, down_mat) + dbias_vec)
    resid_two = resid_one + layer_two * branch_out
    out_img = jnp.where(live[:, None] > 0, resid_two, image_in)
    diff = out_img - teacher_img
    loss_part = jnp.sum(live[:, None] * diff * diff) / (count * D)
    return (out_img, loss_part)

def reference(inputs, teacher, cotangent, token_valid, image_real, w_qkv, q_bias, v_bias, w_out, out_bias, norm1_gain, norm1_bias, scale1, norm2_gain, norm2_bias, w_up, up_bias, w_down, down_bias, scale2):
    params = tuple((arr.astype(jnp.float32) for arr in (w_qkv, q_bias, v_bias, w_out, out_bias, norm1_gain, norm1_bias, scale1, norm2_gain, norm2_bias, w_up, up_bias, w_down, down_bias, scale2)))
    live_all = (token_valid * image_real[:, None]).astype(jnp.float32)
    count = jnp.sum(live_all)

    def one_image(carry, slot):
        grad_sums, loss_sum = carry
        image_in, teacher_img, cot_img, live = slot

        def objective(weights, image_f):
            out_img, loss_part = forward_image(weights, image_f, teacher_img, live, count)
            return (jnp.sum(cot_img * out_img) + loss_part, (out_img, loss_part))
        total_obj, pull_back, (out_img, loss_part) = jax.vjp(objective, params, image_in, has_aux=True)
        weight_grads, input_grad = pull_back(jnp.ones_like(total_obj))
        new_sums = jax.tree.map(lambda left, right: left + right, grad_sums, weight_grads)
        return ((new_sums, loss_sum + loss_part), (out_img.astype(jnp.bfloat16), input_grad))
    init_grads = jax.tree.map(jnp.zeros_like, params)
    slots_in = (inputs.astype(jnp.float32), teacher.astype(jnp.float32), cotangent.astype(jnp.float32), live_all)
    (grad_sums, loss), (result, grad_inputs) = lax.scan(one_image, (init_grads, jnp.zeros((), jnp.float32)), slots_in)
    return (result, loss, grad_inputs) + tuple(grad_sums)
```

```python
import jax
import jax.numpy as jnp
from jax import lax
from jax.experimental import pallas as pl
from jax.experimental.pallas import tpu as pltpu
from jax.sharding import PartitionSpec as P

HEAD_DIM = 64
DEAD = -1000000000.0
SPAN = 352
F32 = jnp.float32
BF16 = jnp.bfloat16
NT = (((1,), (1,)), ((), ()))


def lane_masks(dtype):
    lane = lax.broadcasted_iota(jnp.int32, (1, 2 * HEAD_DIM), 1)
    low = jnp.where(lane < HEAD_DIM, 1.0, 0.0).astype(F32)
    return low.astype(dtype), (1.0 - low).astype(dtype)


def forward_kernel(
    q_own, k_own, v_own, q_rec, k_rec, v_rec, bias_ref, o_own, o_rec, lse_ref, q_s, k_s, v_s, o_s, lse_s
):
    half = q_own.shape[0]
    for all_ref, own, rec in ((q_s, q_own, q_rec), (k_s, k_own, k_rec), (v_s, v_own, v_rec)):
        all_ref[:half, :] = own[...]
        all_ref[half:, :] = rec[...]
    masks = lane_masks(BF16)
    low, high = lane_masks(F32)
    bias = bias_ref[...]

    def block(idx, carry):
        row = pl.multiple_of(idx * SPAN, 16)
        query = q_s[pl.ds(row, SPAN), :]
        outs = []
        sums = []
        for mask in masks:
            scores = lax.dot_general(query * mask, k_s[...], NT, preferred_element_type=F32) + bias
            peak = jnp.max(scores, axis=-1, keepdims=True)
            weight = jnp.exp(scores - peak)
            total = jnp.sum(weight, axis=-1, keepdims=True)
            mixed = jnp.dot(weight.astype(BF16), v_s[...], preferred_element_type=F32)
            outs.append(mixed / total)
            sums.append(peak + jnp.log(total))
        o_s[pl.ds(row, SPAN), :] = (outs[0] * low + outs[1] * high).astype(BF16)
        lse_s[pl.ds(row, SPAN), :] = sums[0] * low + sums[1] * high
        return carry

    lax.fori_loop(0, 2 * half // SPAN, block, 0)
    o_own[...] = o_s[:half, :]
    o_rec[...] = o_s[half:, :]
    turned = jnp.transpose(lse_s[...])
    lse_ref[0, 0:8, :] = turned[0:8, :]
    lse_ref[0, 8:16, :] = turned[HEAD_DIM : HEAD_DIM + 8, :]


def backward_kernel(
    q_own,
    k_own,
    v_own,
    q_rec,
    k_rec,
    v_rec,
    g_own,
    g_rec,
    o_own,
    o_rec,
    lse_ref,
    bias_ref,
    dq_own,
    dk_own,
    dv_own,
    dq_rec,
    dk_rec,
    dv_rec,
    q_s,
    k_s,
    v_s,
    g_s,
    dqt_s,
    dk_s,
    dv_s,
):
    half = q_own.shape[0]
    low, high = lane_masks(BF16)
    for all_ref, own, rec in ((k_s, k_own, k_rec), (v_s, v_own, v_rec)):
        all_ref[:half, :] = own[...]
        all_ref[half:, :] = rec[...]
    for all_ref, own, rec in ((q_s, q_own, q_rec), (g_s, g_own, g_rec)):
        for head, mask in enumerate((low, high)):
            all_ref[head, :half, :] = own[...] * mask
            all_ref[head, half:, :] = rec[...] * mask
    dots_own = jnp.transpose(g_own[...].astype(F32) * o_own[...].astype(F32))
    dots_rec = jnp.transpose(g_rec[...].astype(F32) * o_rec[...].astype(F32))
    dots = jnp.concatenate([dots_own, dots_rec], axis=1)
    inner = (
        jnp.sum(dots[:HEAD_DIM], axis=0, keepdims=True),
        jnp.sum(dots[HEAD_DIM:], axis=0, keepdims=True),
    )
    dqt_s[...] = jnp.zeros_like(dqt_s)

    def block(idx, carry):
        row = pl.multiple_of(idx * SPAN, 16)
        key = k_s[pl.ds(row, SPAN), :]
        value = v_s[pl.ds(row, SPAN), :]
        bias = bias_ref[pl.ds(row, SPAN), :]
        key_t = jnp.transpose(key.astype(F32)).astype(BF16)
        dk = jnp.zeros((SPAN, 2 * HEAD_DIM), F32)
        dv = jnp.zeros((SPAN, 2 * HEAD_DIM), F32)
        for head in range(2):
            query = q_s[head]
            grad = g_s[head]
            lse = lse_ref[0, 8 * head : 8 * head + 1, :]
            prob = jnp.exp(
                lax.dot_general(key, query, NT, preferred_element_type=F32) + bias - lse
            )
            g_prob = lax.dot_general(value, grad, NT, preferred_element_type=F32)
            g_score = (prob * (g_prob - inner[head])).astype(BF16)
            dv = dv + jnp.dot(prob.astype(BF16), grad, preferred_element_type=F32)
            dk = dk + jnp.dot(g_score, query, preferred_element_type=F32)
            rows = slice(HEAD_DIM * head, HEAD_DIM * (head + 1))
            dqt_s[rows, :] += jnp.dot(key_t[rows, :], g_score, preferred_element_type=F32)
        dk_s[pl.ds(row, SPAN), :] = dk.astype(BF16)
        dv_s[pl.ds(row, SPAN), :] = dv.astype(BF16)
        return carry

    lax.fori_loop(0, 2 * half // SPAN, block, 0)
    dq = (jnp.transpose(dqt_s[...]) * HEAD_DIM ** (-0.5)).astype(BF16)
    dq_own[...] = dq[:half, :]
    dq_rec[...] = dq[half:, :]
    for all_ref, own, rec in ((dk_s, dk_own, dk_rec), (dv_s, dv_own, dv_rec)):
        own[...] = all_ref[:half, :]
        rec[...] = all_ref[half:, :]


def pair_blocks(half, pairs):
    wide = 2 * HEAD_DIM
    return [
        pl.BlockSpec((half, wide), lambda pair, part=part: (0, part * pairs + pair))
        for part in range(3)
    ]


def attention(own, rec, bias):
    half = own.shape[0]
    width = own.shape[1] // 3
    wide = 2 * HEAD_DIM
    pairs = width // wide
    full = 2 * half
    col = pl.BlockSpec((half, wide), lambda pair: (0, pair))
    ops = pairs * 2 * full * full
    return pl.pallas_call(
        forward_kernel,
        grid=(pairs,),
        in_specs=pair_blocks(half, pairs)
        + pair_blocks(half, pairs)
        + [pl.BlockSpec((1, full), lambda pair: (0, 0))],
        out_specs=[col, col, pl.BlockSpec((1, 16, full), lambda pair: (pair, 0, 0))],
        out_shape=[
            jax.ShapeDtypeStruct((half, width), BF16),
            jax.ShapeDtypeStruct((half, width), BF16),
            jax.ShapeDtypeStruct((pairs, 16, full), F32),
        ],
        scratch_shapes=[pltpu.VMEM((full, wide), BF16)] * 4 + [pltpu.VMEM((full, wide), F32)],
        cost_estimate=pl.CostEstimate(
            flops=ops * 4 * 256, transcendentals=ops, bytes_accessed=own.size * 6
        ),
        compiler_params=pltpu.CompilerParams(vmem_limit_bytes=56 * 1024 * 1024),
        name="attend",
    )(own, own, own, rec, rec, rec, bias.reshape(1, full))


def attention_back(own, rec, g_own, g_rec, o_own, o_rec, lse, bias):
    half = own.shape[0]
    width = own.shape[1] // 3
    wide = 2 * HEAD_DIM
    pairs = width // wide
    full = 2 * half
    col = pl.BlockSpec((half, wide), lambda pair: (0, pair))
    ops = pairs * 2 * full * full
    return pl.pallas_call(
        backward_kernel,
        grid=(pairs,),
        in_specs=pair_blocks(half, pairs)
        + pair_blocks(half, pairs)
        + [
            col,
            col,
            col,
            col,
            pl.BlockSpec((1, 16, full), lambda pair: (pair, 0, 0)),
            pl.BlockSpec((full, 1), lambda pair: (0, 0)),
        ],
        out_specs=[col] * 6,
        out_shape=[jax.ShapeDtypeStruct((half, width), BF16)] * 6,
        scratch_shapes=[
            pltpu.VMEM((2, full, wide), BF16),
            pltpu.VMEM((full, wide), BF16),
            pltpu.VMEM((full, wide), BF16),
            pltpu.VMEM((2, full, wide), BF16),
            pltpu.VMEM((wide, full), F32),
            pltpu.VMEM((full, wide), BF16),
            pltpu.VMEM((full, wide), BF16),
        ],
        cost_estimate=pl.CostEstimate(
            flops=ops * 10 * 256, transcendentals=ops, bytes_accessed=own.size * 12
        ),
        compiler_params=pltpu.CompilerParams(vmem_limit_bytes=56 * 1024 * 1024),
        name="attend_back",
    )(own, own, own, rec, rec, rec, g_own, g_rec, o_own, o_rec, lse, bias.reshape(full, 1))


def gelu_parts(values):
    phi_sum = 0.5 * (1.0 + lax.erf(values * 0.7071067811865476))
    phi = jnp.exp(-0.5 * values * values) * 0.3989422804014327
    return phi_sum, phi


def norm_parts(values):
    center = values - jnp.mean(values, axis=-1, keepdims=True)
    spread = jnp.mean(center * center, axis=-1, keepdims=True)
    scale = lax.rsqrt(spread + 1e-06)
    return center * scale, scale


def norm_back(values, gain, grad):
    unit, scale = norm_parts(values)
    scaled = grad * gain
    drift = jnp.mean(scaled, axis=-1, keepdims=True)
    slope = jnp.mean(scaled * unit, axis=-1, keepdims=True)
    back = scale * (scaled - drift - unit * slope)
    return back, jnp.sum(grad * unit, axis=0), jnp.sum(grad, axis=0)


def make_step(n_shard, n_seq):
    def place(shard, seq):
        return shard * n_seq + seq

    def route(turn):
        moves = []
        for shard in range(n_shard):
            for seq in range(n_seq):
                src = place(shard, seq)
                dst = place(
                    shard // 2 * 2 + seq % 2, 2 * (shard % 2) + (turn + seq // 2) % 2
                )
                moves.append((src, dst))
        return moves

    there = (route(0), route(1))
    back = tuple([(dst, src) for src, dst in moves] for moves in there)
    swap = [
        (place(shard, seq), place(shard ^ 1, seq))
        for shard in range(n_shard)
        for seq in range(n_seq)
    ]
    axes = ("shard", "seq")

    def on_device(
        inputs,
        teacher,
        cotangent,
        token_valid,
        image_real,
        w_qkv,
        q_bias,
        v_bias,
        w_out,
        out_bias,
        norm1_gain,
        norm1_bias,
        scale1,
        norm2_gain,
        norm2_bias,
        w_up,
        up_bias,
        w_down,
        down_bias,
        scale2,
    ):
        images, tok_dev, width = inputs.shape
        dl = q_bias.shape[0]
        ups = up_bias.shape[0] // dl
        ff = ups * width
        shard_pos = lax.axis_index("shard")
        seq_pos = lax.axis_index("seq")
        core = shard_pos % 2
        turn_out = seq_pos // 2
        turn_in = seq_pos % 2
        pad = SPAN - tok_dev
        rows = 2 * SPAN

        def bring(array):
            got = [
                lax.ppermute(
                    lax.dynamic_index_in_dim(array, (turn + turn_out) % 2, 0, keepdims=False),
                    axes,
                    there[turn],
                )
                for turn in range(2)
            ]
            first = jnp.where(turn_in == 0, got[0], got[1])
            second = jnp.where(turn_in == 0, got[1], got[0])
            both = jnp.stack([first, second])
            return jnp.pad(both, ((0, 0), (0, pad), (0, 0))).reshape(rows, array.shape[-1])

        def give(array):
            parts = array.reshape(2, SPAN, array.shape[-1])[:, :tok_dev]
            got = [
                lax.ppermute(
                    lax.dynamic_index_in_dim(parts, (turn + seq_pos) % 2, 0, keepdims=False),
                    axes,
                    back[turn],
                )
                for turn in range(2)
            ]
            first = jnp.where(turn_out == 0, got[0], got[1])
            second = jnp.where(turn_out == 0, got[1], got[0])
            return jnp.stack([first, second])

        def exchange(array):
            return lax.ppermute(array, axes, swap)

        lengths = jnp.sum(token_valid, axis=1) * image_real
        sizes = jnp.stack([lengths // 64, lengths % 64], axis=1).reshape(1, 2 * images)
        sizes = jnp.pad(sizes.astype(BF16), ((0, 0), (0, dl - 2 * images)))
        small = jnp.concatenate(
            [
                jnp.stack(
                    [
                        q_bias,
                        v_bias,
                        out_bias,
                        norm1_gain,
                        norm1_bias,
                        scale1,
                        norm2_gain,
                        norm2_bias,
                        down_bias,
                        scale2,
                    ]
                ),
                up_bias.reshape(ups, dl),
                sizes,
            ],
            axis=0,
        )
        vecs = lax.all_gather(small, "shard", axis=1, tiled=True).astype(F32)
        qbias, vbias, obias, gain1, shift1, layer1, gain2, shift2, dbias, layer2 = (
            vecs[i] for i in range(10)
        )
        ubias = (
            vecs[10 : 10 + ups].reshape(ups, n_shard, dl).transpose(1, 0, 2).reshape(ff)
        )
        tails = vecs[10 + ups].reshape(n_shard, dl)[:, : 2 * images].reshape(n_shard, images, 2)
        all_len = tails[:, :, 0] * 64.0 + tails[:, :, 1]
        count = jnp.sum(all_len)
        my_len = all_len.reshape(-1)[
            (shard_pos // 2 * 2 + seq_pos // 2) * images + seq_pos % 2
        ]

        slot = jnp.arange(rows)
        offset = slot % SPAN

        def live_of(which):
            token = (which + 2 * (slot // SPAN)) * tok_dev + offset
            return (offset < tok_dev) & (token.astype(F32) < my_len)

        live = live_of(core)
        live_all = jnp.concatenate([live, live_of(1 - core)])
        key_bias = jnp.where(live_all, 0.0, DEAD).astype(F32)
        live = live[:, None]

        qkv_mat = lax.all_gather(w_qkv, "shard", axis=0, tiled=True)
        out_mat = lax.all_gather(w_out, "shard", axis=0, tiled=True)
        up_mat = lax.all_gather(w_up, "shard", axis=0, tiled=True)
        down_mat = lax.all_gather(w_down, "shard", axis=0, tiled=True)

        x_rows = bring(inputs).astype(F32)
        normed1 = (norm_parts(x_rows)[0] * gain1 + shift1).astype(BF16)
        qkv_bias = jnp.concatenate([qbias, jnp.zeros_like(qbias), vbias])
        qkv = (jnp.dot(normed1, qkv_mat, preferred_element_type=F32) + qkv_bias).astype(BF16)
        teacher, cotangent, qkv = lax.optimization_barrier((teacher, cotangent, qkv))
        teach_rows = bring(teacher).astype(F32)
        cot_rows = bring(cotangent).astype(F32)
        head_cols = width // 2

        def parted(array, parts):
            array = array.reshape(rows, parts, 2, head_cols)
            left = array[:, :, 0].reshape(rows, parts * head_cols)
            right = array[:, :, 1].reshape(rows, parts * head_cols)
            return jnp.where(core == 0, left, right), jnp.where(core == 0, right, left)

        def joined(mine, other):
            return jnp.where(core == 0, mine, other), jnp.where(core == 0, other, mine)

        scale = jnp.concatenate(
            [jnp.full((width,), HEAD_DIM ** (-0.5), BF16), jnp.ones((2 * width,), BF16)]
        )
        own, away = parted(qkv * scale, 3)
        rec = exchange(away)
        o_own, o_rec, lse = attention(own, rec, key_bias)
        mixed = jnp.concatenate(joined(o_own, exchange(o_rec)), axis=1)
        attn_out = jnp.dot(mixed, out_mat, preferred_element_type=F32) + obias
        resid1 = x_rows + layer1 * attn_out
        normed2 = (norm_parts(resid1)[0] * gain2 + shift2).astype(BF16)
        pre = jnp.dot(normed2, up_mat, preferred_element_type=F32) + ubias
        act = (pre * gelu_parts(pre)[0]).astype(BF16)
        branch = jnp.dot(act, down_mat, preferred_element_type=F32) + dbias
        resid2 = resid1 + layer2 * branch
        out_rows = jnp.where(live, resid2, x_rows)
        diff = jnp.where(live, out_rows - teach_rows, 0.0)
        err = jnp.sum(diff * diff)
        result = give(out_rows.astype(BF16))

        g_out = cot_rows + 2.0 * diff / (count * width)
        g_keep = jnp.where(live, g_out, 0.0)
        g_pass = g_out - g_keep
        d_scale2 = jnp.sum(g_keep * branch, axis=0)
        g_branch = (g_keep * layer2).astype(BF16)
        d_down_bias = jnp.sum(g_branch.astype(F32), axis=0)

        def weight_grad(left, right):
            return jnp.einsum("ra,rb->ab", left, right, preferred_element_type=F32).astype(BF16)

        def scatter(array):
            return lax.psum_scatter(array, "shard", scatter_dimension=0, tiled=True)

        p_down = scatter(weight_grad(act, g_branch))
        g_hidden = jnp.einsum("rd,fd->rf", g_branch, down_mat, preferred_element_type=F32)
        phi_sum, phi = gelu_parts(pre)
        g_pre = (g_hidden * (phi_sum + pre * phi)).astype(BF16)
        d_up_bias = jnp.sum(g_pre.astype(F32), axis=0)
        p_up = scatter(weight_grad(normed2, g_pre))
        g_norm2 = jnp.einsum("rf,df->rd", g_pre, up_mat, preferred_element_type=F32)
        g_ln2, d_gain2, d_shift2 = norm_back(resid1, gain2, g_norm2)
        g_resid1 = g_keep + g_ln2
        d_scale1 = jnp.sum(g_resid1 * attn_out, axis=0)
        g_attn = (g_resid1 * layer1).astype(BF16)
        d_out_bias = jnp.sum(g_attn.astype(F32), axis=0)
        g_mixed = jnp.einsum("rd,cd->rc", g_attn, out_mat, preferred_element_type=F32).astype(BF16)
        g_mine, g_away = parted(g_mixed, 1)
        g_rec = exchange(g_away)
        p_out = scatter(weight_grad(mixed, g_attn))
        grads = attention_back(own, rec, g_mine, g_rec, o_own, o_rec, lse, key_bias)
        pieces = []
        for part in range(3):
            pieces.extend(joined(grads[part], exchange(grads[3 + part])))
        g_qkv = jnp.concatenate(pieces, axis=1)
        p_qkv = scatter(weight_grad(normed1, g_qkv))
        d_qkv_bias = jnp.sum(g_qkv.astype(F32), axis=0)
        g_norm1 = jnp.einsum("re,de->rd", g_qkv, qkv_mat, preferred_element_type=F32)
        g_ln1, d_gain1, d_shift1 = norm_back(x_rows, gain1, g_norm1)
        g_in = give((g_pass + g_resid1 + g_ln1).astype(BF16)).astype(F32)

        p_down, p_up, p_out = lax.psum((p_down, p_up, p_out), "seq")
        p_qkv = lax.psum(p_qkv, "seq")
        sums = jnp.concatenate(
            [
                jnp.stack(
                    [
                        d_qkv_bias[:width],
                        d_qkv_bias[2 * width :],
                        d_out_bias,
                        d_gain1,
                        d_shift1,
                        d_scale1,
                        d_gain2,
                        d_shift2,
                        d_down_bias,
                        d_scale2,
                    ]
                ),
                d_up_bias.reshape(n_shard, ups, dl).transpose(1, 0, 2).reshape(ups, width),
                jnp.full((1, width), err),
            ],
            axis=0,
        )
        sums = lax.psum(sums, axes)
        loss = sums[10 + ups, 0] / (count * width)
        mine = lax.dynamic_slice_in_dim(sums, shard_pos * dl, dl, 1)
        (
            s_qb, s_vb, s_ob, s_g1, s_b1, s_l1, s_g2, s_b2, s_db, s_l2
        ) = (mine[i] for i in range(10))
        s_ub = mine[10 : 10 + ups].reshape(ups * dl)
        return (
            result,
            loss,
            g_in,
            p_qkv.astype(F32),
            s_qb,
            s_vb,
            p_out.astype(F32),
            s_ob,
            s_g1,
            s_b1,
            s_l1,
            s_g2,
            s_b2,
            p_up.astype(F32),
            s_ub,
            p_down.astype(F32),
            s_db,
            s_l2,
        )

    return on_device


def solution(mesh):
    tokens = P("shard", "seq", None)
    matrix = P("shard", None)
    vector = P("shard")
    in_specs = (
        tokens,
        tokens,
        tokens,
        matrix,
        vector,
        matrix,
        vector,
        vector,
        matrix,
        vector,
        vector,
        vector,
        vector,
        vector,
        vector,
        matrix,
        vector,
        matrix,
        vector,
        vector,
    )
    out_specs = (
        tokens,
        P(),
        tokens,
        matrix,
        vector,
        vector,
        matrix,
        vector,
        vector,
        vector,
        vector,
        vector,
        vector,
        matrix,
        vector,
        matrix,
        vector,
        vector,
    )
    return jax.shard_map(
        make_step(mesh.shape["shard"], mesh.shape["seq"]),
        mesh=mesh,
        in_specs=in_specs,
        out_specs=out_specs,
        check_vma=False,
    )
```

```python
import functools

import jax
import jax.numpy as jnp
from jax import lax
from jax.experimental import pallas as pl
from jax.experimental.pallas import tpu as pltpu
from jax.sharding import PartitionSpec as P

HEAD_DIM = 64
DEAD = -1000000000.0
SPAN = 352
F32 = jnp.float32
BF16 = jnp.bfloat16
NT = (((1,), (1,)), ((), ()))
TN = (((0,), (0,)), ((), ()))


def lane_masks(dtype):
    lane = lax.broadcasted_iota(jnp.int32, (1, 2 * HEAD_DIM), 1)
    low = jnp.where(lane < HEAD_DIM, 1.0, 0.0).astype(F32)
    return low.astype(dtype), (1.0 - low).astype(dtype)


def forward_kernel(
    core_ref, q_own, k_own, v_own, q_rec, k_rec, v_rec, bias_ref, o_ref, lse_ref, q_s, k_s, v_s, lse_s
):
    half = q_own.shape[0]
    for all_ref, own, rec in ((q_s, q_own, q_rec), (k_s, k_own, k_rec), (v_s, v_own, v_rec)):
        all_ref[:half, :] = own[...]
        all_ref[half:, :] = rec[...]
    masks = lane_masks(BF16)
    low, high = lane_masks(F32)
    bias = bias_ref[...]

    def block(idx, carry):
        row = pl.multiple_of(idx * SPAN, 16)
        query = q_s[pl.ds(row, SPAN), :]
        outs = []
        sums = []
        for mask in masks:
            scores = lax.dot_general(query * mask, k_s[...], NT, preferred_element_type=F32) + bias
            peak = jnp.max(scores, axis=-1, keepdims=True)
            weight = jnp.exp(scores - peak)
            total = jnp.sum(weight, axis=-1, keepdims=True)
            mixed = jnp.dot(weight.astype(BF16), v_s[...], preferred_element_type=F32)
            outs.append(mixed / total)
            sums.append(peak + jnp.log(total))
        o_ref[pl.ds(row, SPAN), :] = (outs[0] * low + outs[1] * high).astype(BF16)
        lse_s[pl.ds(row, SPAN), :] = sums[0] * low + sums[1] * high
        return carry

    lax.fori_loop(0, 2 * half // SPAN, block, 0)
    turned = jnp.transpose(lse_s[...])
    lse_ref[0, 0:8, :] = turned[0:8, :]
    lse_ref[0, 8:16, :] = turned[HEAD_DIM : HEAD_DIM + 8, :]


def backward_kernel(
    core_ref,
    q_own,
    k_own,
    v_own,
    q_rec,
    k_rec,
    v_rec,
    g_own,
    g_rec,
    o_ref,
    lse_ref,
    bias_ref,
    *rest,
):
    d_ref, q_s, k_s, v_s, g_s, dqt_s = rest[-6:]
    half = q_own.shape[0]
    width = d_ref.shape[1] // 3
    pair = pl.program_id(0)
    cols = [pl.multiple_of(part * width + pair * 2 * HEAD_DIM, 128) for part in range(3)]
    low, high = lane_masks(BF16)
    for all_ref, own, rec in ((k_s, k_own, k_rec), (v_s, v_own, v_rec)):
        all_ref[:half, :] = own[...]
        all_ref[half:, :] = rec[...]
    for all_ref, own, rec in ((q_s, q_own, q_rec), (g_s, g_own, g_rec)):
        for head, mask in enumerate((low, high)):
            all_ref[head, :half, :] = own[...] * mask
            all_ref[head, half:, :] = rec[...] * mask
    dots_own = jnp.transpose(g_own[...].astype(F32) * o_ref[:half, :].astype(F32))
    dots_rec = jnp.transpose(g_rec[...].astype(F32) * o_ref[half:, :].astype(F32))
    dots = jnp.concatenate([dots_own, dots_rec], axis=1)
    inner = (
        jnp.sum(dots[:HEAD_DIM], axis=0, keepdims=True),
        jnp.sum(dots[HEAD_DIM:], axis=0, keepdims=True),
    )
    dqt_s[...] = jnp.zeros_like(dqt_s)

    def block(idx, carry):
        row = pl.multiple_of(idx * SPAN, 16)
        key = k_s[pl.ds(row, SPAN), :]
        value = v_s[pl.ds(row, SPAN), :]
        bias = bias_ref[pl.ds(row, SPAN), :]
        key_t = jnp.transpose(key.astype(F32)).astype(BF16)
        dk = jnp.zeros((SPAN, 2 * HEAD_DIM), F32)
        dv = jnp.zeros((SPAN, 2 * HEAD_DIM), F32)
        for head in range(2):
            query = q_s[head]
            grad = g_s[head]
            lse = lse_ref[0, 8 * head : 8 * head + 1, :]
            prob = jnp.exp(
                lax.dot_general(key, query, NT, preferred_element_type=F32) + bias - lse
            )
            g_prob = lax.dot_general(value, grad, NT, preferred_element_type=F32)
            g_score = (prob * (g_prob - inner[head])).astype(BF16)
            dv = dv + jnp.dot(prob.astype(BF16), grad, preferred_element_type=F32)
            dk = dk + jnp.dot(g_score, query, preferred_element_type=F32)
            rows = slice(HEAD_DIM * head, HEAD_DIM * (head + 1))
            dqt_s[rows, :] += jnp.dot(key_t[rows, :], g_score, preferred_element_type=F32)
        d_ref[pl.ds(row, SPAN), pl.ds(cols[1], 2 * HEAD_DIM)] = dk.astype(BF16)
        d_ref[pl.ds(row, SPAN), pl.ds(cols[2], 2 * HEAD_DIM)] = dv.astype(BF16)
        return carry

    lax.fori_loop(0, 2 * half // SPAN, block, 0)
    dq = (jnp.transpose(dqt_s[...]) * HEAD_DIM ** (-0.5)).astype(BF16)
    d_ref[:, pl.ds(cols[0], 2 * HEAD_DIM)] = dq


def call(kernel, core, args, grid, in_specs, out_specs, out_shape, scratch, flops, trans):
    moved = sum(arg.size * arg.dtype.itemsize for arg in args)
    return pl.pallas_call(
        kernel,
        grid_spec=pltpu.PrefetchScalarGridSpec(
            num_scalar_prefetch=1,
            grid=grid,
            in_specs=in_specs,
            out_specs=out_specs,
            scratch_shapes=scratch,
        ),
        out_shape=out_shape,
        cost_estimate=pl.CostEstimate(flops=flops, transcendentals=trans, bytes_accessed=moved),
        compiler_params=pltpu.CompilerParams(vmem_limit_bytes=56 * 1024 * 1024),
    )(core, *args)


def head_blocks(half, pairs):
    wide = 2 * HEAD_DIM
    own = [
        pl.BlockSpec((half, wide), lambda pair, core, part=part: (0, 2 * (part * pairs + pair) + core[0]))
        for part in range(3)
    ]
    rec = [
        pl.BlockSpec((half, wide), lambda pair, core, part=part: (0, part * pairs + pair))
        for part in range(3)
    ]
    return own + rec


def attention(core, qkv, rec, bias):
    half = rec.shape[0]
    width = rec.shape[1] // 3
    wide = 2 * HEAD_DIM
    pairs = width // wide
    full = 2 * half
    ops = pairs * 2 * full * full
    return call(
        forward_kernel,
        core,
        (qkv, qkv, qkv, rec, rec, rec, bias.reshape(1, full)),
        (pairs,),
        head_blocks(half, pairs) + [pl.BlockSpec((1, full), lambda pair, core: (0, 0))],
        [
            pl.BlockSpec((full, wide), lambda pair, core: (0, pair)),
            pl.BlockSpec((1, 16, full), lambda pair, core: (pair, 0, 0)),
        ],
        [
            jax.ShapeDtypeStruct((full, width), BF16),
            jax.ShapeDtypeStruct((pairs, 16, full), F32),
        ],
        [pltpu.VMEM((full, wide), BF16)] * 3 + [pltpu.VMEM((full, wide), F32)],
        ops * 4 * 256,
        ops,
    )


def attention_back(core, qkv, rec, g_own, g_rec, mixed, lse, bias, after):
    half = rec.shape[0]
    width = rec.shape[1] // 3
    wide = 2 * HEAD_DIM
    pairs = width // wide
    full = 2 * half
    col = pl.BlockSpec((half, wide), lambda pair, core: (0, pair))
    ops = pairs * 2 * full * full
    return call(
        backward_kernel,
        core,
        (qkv, qkv, qkv, rec, rec, rec, g_own, g_rec, mixed, lse, bias.reshape(full, 1)) + tuple(after),
        (pairs,),
        head_blocks(half, pairs)
        + [
            col,
            col,
            pl.BlockSpec((full, wide), lambda pair, core: (0, pair)),
            pl.BlockSpec((1, 16, full), lambda pair, core: (pair, 0, 0)),
            pl.BlockSpec((full, 1), lambda pair, core: (0, 0)),
        ]
        + [pl.BlockSpec(memory_space=pl.ANY)] * len(after),
        pl.BlockSpec((full, 3 * width), lambda pair, core: (0, 0)),
        jax.ShapeDtypeStruct((full, 3 * width), BF16),
        [
            pltpu.VMEM((2, full, wide), BF16),
            pltpu.VMEM((full, wide), BF16),
            pltpu.VMEM((full, wide), BF16),
            pltpu.VMEM((2, full, wide), BF16),
            pltpu.VMEM((wide, full), F32),
        ],
        ops * 10 * 256,
        ops,
    )


def grad_kernel(core_ref, *refs):
    a_own, a_rec = refs[:2]
    b_rec, out = refs[-2:]
    start = 0
    for b_own in refs[2:-2]:
        cols = slice(start, start + b_own.shape[1])
        total = lax.dot_general(a_own[...], b_own[...], TN, preferred_element_type=F32)
        total += lax.dot_general(a_rec[...], b_rec[:, cols], TN, preferred_element_type=F32)
        out[:, cols] = total.astype(BF16)
        start += b_own.shape[1]


def weight_grad(core, a_own, a_rec, b_owns, b_rec, specs, shape, tile):
    args = (a_own, a_rec) + tuple(b_owns) + (b_rec,)
    rows = 4 * SPAN
    return call(
        grad_kernel,
        core,
        args,
        (shape[0] // tile,),
        specs,
        pl.BlockSpec((tile, shape[1]), lambda i, core: (i, 0)),
        jax.ShapeDtypeStruct(shape, BF16),
        [],
        2 * rows * shape[0] * shape[1],
        0,
    )


def pick_kernel(unit, core_ref, src, dst):
    for parity in range(2):

        @pl.when(core_ref[0] == parity)
        def _():
            for idx in range(dst.shape[1] // unit):
                low = (2 * idx + 1 - parity) * unit
                dst[:, idx * unit : (idx + 1) * unit] = src[:, low : low + unit]


def pick_other(core, array, unit):
    rows, width = array.shape
    wide = 1024
    return call(
        functools.partial(pick_kernel, unit),
        core,
        (array,),
        (width // wide,),
        [pl.BlockSpec((rows, wide), lambda i, core: (0, i))],
        pl.BlockSpec((rows, wide // 2), lambda i, core: (0, i)),
        jax.ShapeDtypeStruct((rows, width // 2), array.dtype),
        [],
        0,
        0,
    )


def merge_kernel(unit, core_ref, own, rec, dst):
    for parity in range(2):

        @pl.when(core_ref[0] == parity)
        def _():
            for idx in range(own.shape[1] // unit):
                cols = slice(idx * unit, (idx + 1) * unit)
                for side, src in enumerate((own, rec)):
                    low = (2 * idx + (parity + side) % 2) * unit
                    dst[:, low : low + unit] = src[:, cols]


def merge(core, own, rec, rows, unit):
    width = rec.shape[1]
    wide = 512
    spec = pl.BlockSpec((rows, wide), lambda i, core: (0, i))
    return call(
        functools.partial(merge_kernel, unit),
        core,
        (own, rec),
        (width // wide,),
        [spec, spec],
        pl.BlockSpec((rows, 2 * wide), lambda i, core: (0, i)),
        jax.ShapeDtypeStruct((rows, 2 * width), rec.dtype),
        [],
        0,
        0,
    )


def gelu_parts(values):
    phi_sum = 0.5 * (1.0 + lax.erf(values * 0.7071067811865476))
    phi = jnp.exp(-0.5 * values * values) * 0.3989422804014327
    return phi_sum, phi


def norm_parts(values):
    center = values - jnp.mean(values, axis=-1, keepdims=True)
    spread = jnp.mean(center * center, axis=-1, keepdims=True)
    scale = lax.rsqrt(spread + 1e-06)
    return center * scale, scale


def norm_back(values, gain, grad):
    unit, scale = norm_parts(values)
    scaled = grad * gain
    drift = jnp.mean(scaled, axis=-1, keepdims=True)
    slope = jnp.mean(scaled * unit, axis=-1, keepdims=True)
    back = scale * (scaled - drift - unit * slope)
    return back, jnp.sum(grad * unit, axis=0), jnp.sum(grad, axis=0)


def make_step(n_shard, n_seq):
    def place(shard, seq):
        return shard * n_seq + seq

    def route(turn):
        moves = []
        for shard in range(n_shard):
            for seq in range(n_seq):
                src = place(shard, seq)
                dst = place(
                    shard // 2 * 2 + seq % 2, 2 * (shard % 2) + (turn + seq // 2) % 2
                )
                moves.append((src, dst))
        return moves

    there = (route(0), route(1))
    back = tuple([(dst, src) for src, dst in moves] for moves in there)
    swap = [
        (place(shard, seq), place(shard ^ 1, seq))
        for shard in range(n_shard)
        for seq in range(n_seq)
    ]
    axes = ("shard", "seq")
    chips = [list(range(core, n_shard, 2)) for core in range(2)]

    def inner(
        inputs,
        teacher,
        cotangent,
        token_valid,
        image_real,
        w_qkv,
        q_bias,
        v_bias,
        w_out,
        out_bias,
        norm1_gain,
        norm1_bias,
        scale1,
        norm2_gain,
        norm2_bias,
        w_up,
        up_bias,
        w_down,
        down_bias,
        scale2,
    ):
        images, tok_dev, width = inputs.shape
        dl = q_bias.shape[0]
        ups = up_bias.shape[0] // dl
        ff = ups * width
        shard_pos = lax.axis_index("shard")
        seq_pos = lax.axis_index("seq")
        core = shard_pos % 2
        turn_out = seq_pos // 2
        turn_in = seq_pos % 2
        pad = SPAN - tok_dev
        rows = 2 * SPAN

        def bring(array):
            got = [
                lax.ppermute(
                    lax.dynamic_index_in_dim(array, (turn + turn_out) % 2, 0, keepdims=False),
                    axes,
                    there[turn],
                )
                for turn in range(2)
            ]
            first = jnp.where(turn_in == 0, got[0], got[1])
            second = jnp.where(turn_in == 0, got[1], got[0])
            both = jnp.stack([first, second])
            return jnp.pad(both, ((0, 0), (0, pad), (0, 0))).reshape(rows, array.shape[-1])

        def give(array):
            parts = array.reshape(2, SPAN, array.shape[-1])[:, :tok_dev]
            got = [
                lax.ppermute(
                    lax.dynamic_index_in_dim(parts, (turn + seq_pos) % 2, 0, keepdims=False),
                    axes,
                    back[turn],
                )
                for turn in range(2)
            ]
            first = jnp.where(turn_out == 0, got[0], got[1])
            second = jnp.where(turn_out == 0, got[1], got[0])
            return jnp.stack([first, second])

        def exchange(array):
            return lax.ppermute(array, axes, swap)

        halves = dl % (2 * HEAD_DIM) == 0

        def interleave(own, other, part, axis):
            own = jnp.split(own, own.shape[axis] // part, axis)
            other = jnp.split(other, len(own), axis)
            blocks = []
            for mine, his in zip(own, other):
                blocks.append(jnp.where(core == 0, mine, his))
                blocks.append(jnp.where(core == 0, his, mine))
            return jnp.concatenate(blocks, axis)

        def scatter(array, part, axis):
            if halves:
                return lax.psum_scatter(
                    array, "shard", scatter_dimension=0, axis_index_groups=chips, tiled=True
                )
            array = interleave(array, jnp.zeros_like(array), part, axis)
            return lax.psum_scatter(array, "shard", scatter_dimension=0, tiled=True)

        def z_reduce(array):
            split = (n_seq, array.shape[0] // n_seq, array.shape[1])
            got = lax.all_to_all(array.reshape(split), "seq", 0, 0, tiled=True)
            total = jnp.sum(got.astype(F32), axis=0).astype(BF16)
            got = lax.all_to_all(
                jnp.broadcast_to(total[None], split), "seq", 0, 0, tiled=True
            )
            return got.reshape(array.shape)

        def spread(array, part):
            if not halves:
                return array
            array = array.reshape(2, dl, array.shape[1])
            keep = lax.dynamic_index_in_dim(array, core, 0, keepdims=False)
            away = lax.dynamic_index_in_dim(array, 1 - core, 0, keepdims=False)
            return interleave(keep, exchange(away), part, 1)

        lengths = jnp.sum(token_valid, axis=1) * image_real
        sizes = jnp.stack([lengths // 64, lengths % 64], axis=1).reshape(1, 2 * images)
        sizes = jnp.pad(sizes.astype(BF16), ((0, 0), (0, dl - 2 * images)))
        small = jnp.concatenate(
            [
                jnp.stack(
                    [
                        q_bias,
                        v_bias,
                        out_bias,
                        norm1_gain,
                        norm1_bias,
                        scale1,
                        norm2_gain,
                        norm2_bias,
                        down_bias,
                        scale2,
                    ]
                ),
                up_bias.reshape(ups, dl),
                sizes,
            ],
            axis=0,
        )
        vecs = lax.all_gather(small, "shard", axis=1, tiled=True).astype(F32)
        qbias, vbias, obias, gain1, shift1, layer1, gain2, shift2, dbias, layer2 = (
            vecs[i] for i in range(10)
        )
        ubias = (
            vecs[10 : 10 + ups].reshape(ups, n_shard, dl).transpose(1, 0, 2).reshape(ff)
        )
        tails = vecs[10 + ups].reshape(n_shard, dl)[:, : 2 * images].reshape(n_shard, images, 2)
        all_len = tails[:, :, 0] * 64.0 + tails[:, :, 1]
        count = jnp.sum(all_len)
        my_len = all_len.reshape(-1)[
            (shard_pos // 2 * 2 + seq_pos // 2) * images + seq_pos % 2
        ]

        slot = jnp.arange(rows)
        offset = slot % SPAN

        def live_of(which):
            token = (which + 2 * (slot // SPAN)) * tok_dev + offset
            return (offset < tok_dev) & (token.astype(F32) < my_len)

        live = live_of(core)
        live_all = jnp.concatenate([live, live_of(1 - core)])
        key_bias = jnp.where(live_all, 0.0, DEAD).astype(F32)
        live = live[:, None]

        qkv_mat = lax.all_gather(w_qkv, "shard", axis=0, tiled=True)
        out_mat = lax.all_to_all(
            jnp.broadcast_to(w_out[None], (n_shard, dl, width)), "shard", 0, 0, tiled=True
        ).reshape(width, width)
        up_mat = lax.all_gather(w_up, "shard", axis=0, tiled=True)
        down_mat = lax.all_gather(w_down, "shard", axis=0, tiled=True)

        unit = 2 * HEAD_DIM
        ff_unit = max(ff // n_shard, 4 * unit)
        core_arr = core.astype(jnp.int32).reshape(1)
        x_rows = bring(inputs).astype(F32)
        normed1 = (norm_parts(x_rows)[0] * gain1 + shift1).astype(BF16)
        normed1_rec = exchange(normed1)
        qkv_bias = jnp.concatenate([qbias, jnp.zeros_like(qbias), vbias])
        scale = jnp.concatenate(
            [jnp.full((width,), HEAD_DIM ** (-0.5), BF16), jnp.ones((2 * width,), BF16)]
        )
        qkv = (jnp.dot(normed1, qkv_mat, preferred_element_type=F32) + qkv_bias).astype(BF16) * scale
        rec = exchange(pick_other(core_arr, qkv, unit))
        mixed_mine, lse = attention(core_arr, qkv, rec, key_bias)
        both = bring(jnp.concatenate([teacher, cotangent], axis=-1))
        teach_rows = both[:, :width].astype(F32)
        cot_rows = both[:, width:].astype(F32)
        mixed = merge(core_arr, mixed_mine, exchange(mixed_mine[rows:]), rows, unit)
        attn_out = jnp.dot(mixed, out_mat, preferred_element_type=F32) + obias
        resid1 = x_rows + layer1 * attn_out
        normed2 = (norm_parts(resid1)[0] * gain2 + shift2).astype(BF16)
        normed2_rec = exchange(normed2)
        pre = jnp.dot(normed2, up_mat, preferred_element_type=F32) + ubias
        act = (pre * gelu_parts(pre)[0]).astype(BF16)
        act_rec = exchange(pick_other(core_arr, act, ff_unit))
        branch = jnp.dot(act, down_mat, preferred_element_type=F32) + dbias
        resid2 = resid1 + layer2 * branch
        out_rows = jnp.where(live, resid2, x_rows)
        diff = jnp.where(live, out_rows - teach_rows, 0.0)
        err = jnp.sum(diff * diff)
        result = give(out_rows.astype(BF16))

        g_out = cot_rows + 2.0 * diff / (count * width)
        g_keep = jnp.where(live, g_out, 0.0)
        g_pass = g_out - g_keep
        d_scale2 = jnp.sum(g_keep * branch, axis=0)
        g_branch = (g_keep * layer2).astype(BF16)
        d_down_bias = jnp.sum(g_branch.astype(F32), axis=0)
        g_branch_rec = exchange(g_branch)

        tile = 2 * unit
        whole = pl.BlockSpec((rows, width), lambda i, core: (0, 0))
        strip = pl.BlockSpec((rows, tile), lambda i, core: (0, i))
        per = ff_unit // tile
        w_down_part = weight_grad(
            core_arr,
            act,
            act_rec,
            (g_branch,),
            g_branch_rec,
            [
                pl.BlockSpec(
                    (rows, tile), lambda i, core: (0, (2 * (i // per) + core[0]) * per + i % per)
                ),
                strip,
                whole,
                whole,
            ],
            (ff // 2, width),
            tile,
        )
        p_down = scatter(w_down_part, ff_unit, 0)
        g_hidden = jnp.einsum("rd,fd->rf", g_branch, down_mat, preferred_element_type=F32)
        phi_sum, phi = gelu_parts(pre)
        g_pre = (g_hidden * (phi_sum + pre * phi)).astype(BF16)
        d_up_bias = jnp.sum(g_pre.astype(F32), axis=0)
        g_pre_rec = exchange(pick_other(core_arr, g_pre, ff_unit))
        n_units = ff // ff_unit // 2
        w_up_part = weight_grad(
            core_arr,
            normed2,
            normed2_rec,
            (g_pre,) * n_units,
            g_pre_rec,
            [strip, strip]
            + [
                pl.BlockSpec((rows, ff_unit), lambda i, core, j=j: (0, 2 * j + core[0]))
                for j in range(n_units)
            ]
            + [pl.BlockSpec((rows, ff // 2), lambda i, core: (0, 0))],
            (width, ff // 2),
            tile,
        )
        p_up = scatter(w_up_part, ff_unit, 1)
        g_norm2 = jnp.einsum("rf,df->rd", g_pre, up_mat, preferred_element_type=F32)
        g_ln2, d_gain2, d_shift2 = norm_back(resid1, gain2, g_norm2)
        g_resid1 = g_keep + g_ln2
        d_scale1 = jnp.sum(g_resid1 * attn_out, axis=0)
        g_attn = (g_resid1 * layer1).astype(BF16)
        d_out_bias = jnp.sum(g_attn.astype(F32), axis=0)
        g_attn_rec = exchange(g_attn)
        out_mine = lax.dynamic_index_in_dim(
            out_mat.reshape(width // unit // 2, 2, unit, width), core, 1, keepdims=False
        ).reshape(width // 2, width)

        def mixed_grad(array):
            return jnp.einsum("rd,cd->rc", array, out_mine, preferred_element_type=F32).astype(BF16)

        w_out_part = weight_grad(
            core_arr,
            mixed_mine,
            mixed_mine,
            (g_attn,),
            g_attn_rec,
            [strip, pl.BlockSpec((rows, tile), lambda i, core: (1, i)), whole, whole],
            (width // 2, width),
            tile,
        )
        p_out = scatter(w_out_part, unit, 0)
        g_all = attention_back(
            core_arr,
            qkv,
            rec,
            mixed_grad(g_attn),
            mixed_grad(g_attn_rec),
            mixed_mine,
            lse,
            key_bias,
            (),
        )
        g_rec = exchange(g_all[rows:])
        w_qkv_part = weight_grad(
            core_arr,
            normed1,
            normed1_rec,
            (g_all,),
            g_all,
            [
                strip,
                strip,
                pl.BlockSpec((rows, 3 * width // 2), lambda i, core: (0, 0)),
                pl.BlockSpec((rows, 3 * width // 2), lambda i, core: (1, 0)),
            ],
            (width, 3 * width // 2),
            tile,
        )
        p_qkv = scatter(w_qkv_part, unit, 1)
        g_qkv = merge(core_arr, g_all, g_rec, rows, unit)
        d_qkv_bias = jnp.sum(g_qkv.astype(F32), axis=0)
        g_norm1 = jnp.einsum("re,de->rd", g_qkv, qkv_mat, preferred_element_type=F32)
        g_ln1, d_gain1, d_shift1 = norm_back(x_rows, gain1, g_norm1)
        g_in = give((g_pass + g_resid1 + g_ln1).astype(BF16)).astype(F32)

        p_down = z_reduce(p_down)
        p_up = z_reduce(p_up)
        p_out, p_qkv = lax.psum((p_out, p_qkv), "seq")
        p_up = spread(p_up, ff_unit)
        p_qkv = spread(p_qkv, unit)
        sums = jnp.concatenate(
            [
                jnp.stack(
                    [
                        d_qkv_bias[:width],
                        d_qkv_bias[2 * width :],
                        d_out_bias,
                        d_gain1,
                        d_shift1,
                        d_scale1,
                        d_gain2,
                        d_shift2,
                        d_down_bias,
                        d_scale2,
                    ]
                ),
                d_up_bias.reshape(n_shard, ups, dl).transpose(1, 0, 2).reshape(ups, width),
                jnp.full((1, width), err),
            ],
            axis=0,
        )
        kinds = sums.shape[0]
        sums = sums.reshape(kinds, n_shard, 1, dl).transpose(1, 2, 0, 3)
        sums = jnp.broadcast_to(sums, (n_shard, n_seq, kinds, dl))
        sums = lax.all_to_all(
            sums.reshape(n_shard * n_seq, kinds, dl), axes, 0, 0, tiled=True
        )
        mine = jnp.sum(sums, axis=0)
        loss = mine[10 + ups, 0] / (count * width)
        (
            s_qb, s_vb, s_ob, s_g1, s_b1, s_l1, s_g2, s_b2, s_db, s_l2
        ) = (mine[i] for i in range(10))
        s_ub = mine[10 : 10 + ups].reshape(ups * dl)
        return (
            result,
            loss,
            g_in,
            p_qkv.astype(F32),
            s_qb,
            s_vb,
            p_out.astype(F32),
            s_ob,
            s_g1,
            s_b1,
            s_l1,
            s_g2,
            s_b2,
            p_up.astype(F32),
            s_ub,
            p_down.astype(F32),
            s_db,
            s_l2,
        )

    return inner


def solution(mesh):
    tokens = P("shard", "seq", None)
    matrix = P("shard", None)
    vector = P("shard")
    in_specs = (
        tokens,
        tokens,
        tokens,
        matrix,
        vector,
        matrix,
        vector,
        vector,
        matrix,
        vector,
        vector,
        vector,
        vector,
        vector,
        vector,
        matrix,
        vector,
        matrix,
        vector,
        vector,
    )
    out_specs = (
        tokens,
        P(),
        tokens,
        matrix,
        vector,
        vector,
        matrix,
        vector,
        vector,
        vector,
        vector,
        vector,
        vector,
        matrix,
        vector,
        matrix,
        vector,
        vector,
    )
    return jax.shard_map(
        make_step(mesh.shape["shard"], mesh.shape["seq"]),
        mesh=mesh,
        in_specs=in_specs,
        out_specs=out_specs,
        check_vma=False,
    )
```

```python
import functools

import jax
import jax.numpy as jnp
from jax import lax
from jax.experimental import pallas as pl
from jax.experimental.pallas import tpu as pltpu
from jax.sharding import PartitionSpec as P

HEAD_DIM = 64
DEAD = -1000000000.0
SPAN = 352
F32 = jnp.float32
BF16 = jnp.bfloat16
NT = (((1,), (1,)), ((), ()))
TN = (((0,), (0,)), ((), ()))


def lane_masks(dtype):
    lane = lax.broadcasted_iota(jnp.int32, (1, 2 * HEAD_DIM), 1)
    low = jnp.where(lane < HEAD_DIM, 1.0, 0.0).astype(F32)
    return low.astype(dtype), (1.0 - low).astype(dtype)


def forward_kernel(
    core_ref, q_own, k_own, v_own, q_rec, k_rec, v_rec, bias_ref, o_ref, lse_ref, q_s, k_s, v_s, lse_s
):
    half = q_own.shape[0]
    for all_ref, own, rec in ((q_s, q_own, q_rec), (k_s, k_own, k_rec), (v_s, v_own, v_rec)):
        all_ref[:half, :] = own[...]
        all_ref[half:, :] = rec[...]
    masks = lane_masks(BF16)
    low, high = lane_masks(F32)
    bias = bias_ref[...]

    def block(idx, carry):
        row = pl.multiple_of(idx * SPAN, 16)
        query = q_s[pl.ds(row, SPAN), :]
        outs = []
        sums = []
        for mask in masks:
            scores = lax.dot_general(query * mask, k_s[...], NT, preferred_element_type=F32) + bias
            peak = jnp.max(scores, axis=-1, keepdims=True)
            weight = jnp.exp(scores - peak)
            total = jnp.sum(weight, axis=-1, keepdims=True)
            mixed = jnp.dot(weight.astype(BF16), v_s[...], preferred_element_type=F32)
            outs.append(mixed / total)
            sums.append(peak + jnp.log(total))
        o_ref[pl.ds(row, SPAN), :] = (outs[0] * low + outs[1] * high).astype(BF16)
        lse_s[pl.ds(row, SPAN), :] = sums[0] * low + sums[1] * high
        return carry

    lax.fori_loop(0, 2 * half // SPAN, block, 0)
    turned = jnp.transpose(lse_s[...])
    lse_ref[0, 0:8, :] = turned[0:8, :]
    lse_ref[0, 8:16, :] = turned[HEAD_DIM : HEAD_DIM + 8, :]


def backward_kernel(
    core_ref,
    q_own,
    k_own,
    v_own,
    q_rec,
    k_rec,
    v_rec,
    g_own,
    g_rec,
    o_ref,
    lse_ref,
    bias_ref,
    d_ref,
    q_s,
    k_s,
    v_s,
    g_s,
    dqt_s,
):
    half = q_own.shape[0]
    width = d_ref.shape[1] // 3
    pair = pl.program_id(0)
    cols = [pl.multiple_of(part * width + pair * 2 * HEAD_DIM, 128) for part in range(3)]
    low, high = lane_masks(BF16)
    for all_ref, own, rec in ((k_s, k_own, k_rec), (v_s, v_own, v_rec)):
        all_ref[:half, :] = own[...]
        all_ref[half:, :] = rec[...]
    for all_ref, own, rec in ((q_s, q_own, q_rec), (g_s, g_own, g_rec)):
        for head, mask in enumerate((low, high)):
            all_ref[head, :half, :] = own[...] * mask
            all_ref[head, half:, :] = rec[...] * mask
    dots_own = jnp.transpose(g_own[...].astype(F32) * o_ref[:half, :].astype(F32))
    dots_rec = jnp.transpose(g_rec[...].astype(F32) * o_ref[half:, :].astype(F32))
    dots = jnp.concatenate([dots_own, dots_rec], axis=1)
    inner = (
        jnp.sum(dots[:HEAD_DIM], axis=0, keepdims=True),
        jnp.sum(dots[HEAD_DIM:], axis=0, keepdims=True),
    )
    dqt_s[...] = jnp.zeros_like(dqt_s)

    def block(idx, carry):
        row = pl.multiple_of(idx * SPAN, 16)
        key = k_s[pl.ds(row, SPAN), :]
        value = v_s[pl.ds(row, SPAN), :]
        bias = bias_ref[pl.ds(row, SPAN), :]
        key_t = jnp.transpose(key.astype(F32)).astype(BF16)
        dk = jnp.zeros((SPAN, 2 * HEAD_DIM), F32)
        dv = jnp.zeros((SPAN, 2 * HEAD_DIM), F32)
        for head in range(2):
            query = q_s[head]
            grad = g_s[head]
            lse = lse_ref[0, 8 * head : 8 * head + 1, :]
            prob = jnp.exp(
                lax.dot_general(key, query, NT, preferred_element_type=F32) + bias - lse
            )
            g_prob = lax.dot_general(value, grad, NT, preferred_element_type=F32)
            g_score = (prob * (g_prob - inner[head])).astype(BF16)
            dv = dv + jnp.dot(prob.astype(BF16), grad, preferred_element_type=F32)
            dk = dk + jnp.dot(g_score, query, preferred_element_type=F32)
            rows = slice(HEAD_DIM * head, HEAD_DIM * (head + 1))
            dqt_s[rows, :] += jnp.dot(key_t[rows, :], g_score, preferred_element_type=F32)
        d_ref[pl.ds(row, SPAN), pl.ds(cols[1], 2 * HEAD_DIM)] = dk.astype(BF16)
        d_ref[pl.ds(row, SPAN), pl.ds(cols[2], 2 * HEAD_DIM)] = dv.astype(BF16)
        return carry

    lax.fori_loop(0, 2 * half // SPAN, block, 0)
    dq = (jnp.transpose(dqt_s[...]) * HEAD_DIM ** (-0.5)).astype(BF16)
    d_ref[:, pl.ds(cols[0], 2 * HEAD_DIM)] = dq


def call(kernel, core, args, grid, in_specs, out_specs, out_shape, scratch, flops, trans):
    moved = sum(arg.size * arg.dtype.itemsize for arg in args)
    return pl.pallas_call(
        kernel,
        grid_spec=pltpu.PrefetchScalarGridSpec(
            num_scalar_prefetch=1,
            grid=grid,
            in_specs=in_specs,
            out_specs=out_specs,
            scratch_shapes=scratch,
        ),
        out_shape=out_shape,
        cost_estimate=pl.CostEstimate(flops=flops, transcendentals=trans, bytes_accessed=moved),
        compiler_params=pltpu.CompilerParams(vmem_limit_bytes=56 * 1024 * 1024),
    )(core, *args)


def head_blocks(half, pairs, first=0):
    wide = 2 * HEAD_DIM
    own = [
        pl.BlockSpec(
            (half, wide),
            lambda pair, core, part=part: (0, 2 * (part * pairs + pair + first) + core[0]),
        )
        for part in range(3)
    ]
    rec = [
        pl.BlockSpec((half, wide), lambda pair, core, part=part: (0, part * pairs + pair + first))
        for part in range(3)
    ]
    return own + rec


def attention(core, qkv, rec, bias):
    half = rec.shape[0]
    width = rec.shape[1] // 3
    wide = 2 * HEAD_DIM
    pairs = width // wide
    full = 2 * half
    ops = pairs * 2 * full * full
    return call(
        forward_kernel,
        core,
        (qkv, qkv, qkv, rec, rec, rec, bias.reshape(1, full)),
        (pairs,),
        head_blocks(half, pairs) + [pl.BlockSpec((1, full), lambda pair, core: (0, 0))],
        [
            pl.BlockSpec((full, wide), lambda pair, core: (0, pair)),
            pl.BlockSpec((1, 16, full), lambda pair, core: (pair, 0, 0)),
        ],
        [
            jax.ShapeDtypeStruct((full, width), BF16),
            jax.ShapeDtypeStruct((pairs, 16, full), F32),
        ],
        [pltpu.VMEM((full, wide), BF16)] * 3 + [pltpu.VMEM((full, wide), F32)],
        ops * 4 * 256,
        ops,
    )


def attention_back(core, qkv, rec, g_own, g_rec, mixed, lse, bias, first, last):
    half = rec.shape[0]
    wide = 2 * HEAD_DIM
    pairs = rec.shape[1] // 3 // wide
    here = last - first
    full = 2 * half
    col = pl.BlockSpec((half, wide), lambda pair, core: (0, pair + first))
    ops = here * 2 * full * full
    return call(
        backward_kernel,
        core,
        (qkv, qkv, qkv, rec, rec, rec, g_own, g_rec, mixed, lse, bias.reshape(full, 1)),
        (here,),
        head_blocks(half, pairs, first)
        + [
            col,
            col,
            pl.BlockSpec((full, wide), lambda pair, core: (0, pair + first)),
            pl.BlockSpec((1, 16, full), lambda pair, core: (pair + first, 0, 0)),
            pl.BlockSpec((full, 1), lambda pair, core: (0, 0)),
        ],
        pl.BlockSpec((full, 3 * here * wide), lambda pair, core: (0, 0)),
        jax.ShapeDtypeStruct((full, 3 * here * wide), BF16),
        [
            pltpu.VMEM((2, full, wide), BF16),
            pltpu.VMEM((full, wide), BF16),
            pltpu.VMEM((full, wide), BF16),
            pltpu.VMEM((2, full, wide), BF16),
            pltpu.VMEM((wide, full), F32),
        ],
        ops * 10 * 256,
        ops,
    )


def grad_kernel(core_ref, a_own, a_rec, *refs):
    out = refs[-1]
    count = len(refs) // 2
    start = 0
    for b_own, b_rec in zip(refs[:count], refs[count:-1]):
        total = lax.dot_general(a_own[...], b_own[...], TN, preferred_element_type=F32)
        total += lax.dot_general(a_rec[...], b_rec[...], TN, preferred_element_type=F32)
        out[:, start : start + b_own.shape[1]] = total.astype(BF16)
        start += b_own.shape[1]


def weight_grad(core, args, specs, shape, tile):
    rows = 4 * SPAN
    return call(
        grad_kernel,
        core,
        args,
        (shape[0] // tile,),
        specs,
        pl.BlockSpec((tile, shape[1]), lambda i, core: (i, 0)),
        jax.ShapeDtypeStruct(shape, BF16),
        [],
        2 * rows * shape[0] * shape[1],
        0,
    )


def pick_kernel(unit, core_ref, src, dst):
    for parity in range(2):

        @pl.when(core_ref[0] == parity)
        def _():
            for idx in range(dst.shape[1] // unit):
                low = (2 * idx + 1 - parity) * unit
                dst[:, idx * unit : (idx + 1) * unit] = src[:, low : low + unit]


def pick_other(core, array, unit):
    rows, width = array.shape
    wide = 1024
    return call(
        functools.partial(pick_kernel, unit),
        core,
        (array,),
        (width // wide,),
        [pl.BlockSpec((rows, wide), lambda i, core: (0, i))],
        pl.BlockSpec((rows, wide // 2), lambda i, core: (0, i)),
        jax.ShapeDtypeStruct((rows, width // 2), array.dtype),
        [],
        0,
        0,
    )


def merge_kernel(unit, core_ref, *refs):
    dst = refs[-1]
    count = len(refs) // 2
    for parity in range(2):

        @pl.when(core_ref[0] == parity)
        def _():
            at = 0
            for own, rec in zip(refs[:count], refs[count:-1]):
                for idx in range(own.shape[1] // unit):
                    cols = slice(idx * unit, (idx + 1) * unit)
                    for side, src in enumerate((own, rec)):
                        low = at + (parity + side) % 2 * unit
                        dst[:, low : low + unit] = src[:, cols]
                    at += 2 * unit


def merge(core, owns, recs, rows, unit, steps):
    width = sum(rec.shape[1] for rec in recs)
    specs = [pl.BlockSpec((rows, rec.shape[1] // steps), lambda i, core: (0, i)) for rec in recs]
    return call(
        functools.partial(merge_kernel, unit),
        core,
        tuple(owns) + tuple(recs),
        (steps,),
        specs + specs,
        pl.BlockSpec((rows, 2 * width // steps), lambda i, core: (0, i)),
        jax.ShapeDtypeStruct((rows, 2 * width), recs[0].dtype),
        [],
        0,
        0,
    )


def gelu_parts(values):
    phi_sum = 0.5 * (1.0 + lax.erf(values * 0.7071067811865476))
    phi = jnp.exp(-0.5 * values * values) * 0.3989422804014327
    return phi_sum, phi


def norm_parts(values):
    center = values - jnp.mean(values, axis=-1, keepdims=True)
    spread = jnp.mean(center * center, axis=-1, keepdims=True)
    scale = lax.rsqrt(spread + 1e-06)
    return center * scale, scale


def norm_back(values, gain, grad):
    unit, scale = norm_parts(values)
    scaled = grad * gain
    drift = jnp.mean(scaled, axis=-1, keepdims=True)
    slope = jnp.mean(scaled * unit, axis=-1, keepdims=True)
    back = scale * (scaled - drift - unit * slope)
    return back, jnp.sum(grad * unit, axis=0), jnp.sum(grad, axis=0)


def make_step(n_shard, n_seq):
    def place(shard, seq):
        return shard * n_seq + seq

    def route(turn):
        moves = []
        for shard in range(n_shard):
            for seq in range(n_seq):
                src = place(shard, seq)
                dst = place(
                    shard // 2 * 2 + seq % 2, 2 * (shard % 2) + (turn + seq // 2) % 2
                )
                moves.append((src, dst))
        return moves

    there = (route(0), route(1))
    back = tuple([(dst, src) for src, dst in moves] for moves in there)
    swap = [
        (place(shard, seq), place(shard ^ 1, seq))
        for shard in range(n_shard)
        for seq in range(n_seq)
    ]
    axes = ("shard", "seq")
    chips = [list(range(core, n_shard, 2)) for core in range(2)]

    def inner(
        inputs,
        teacher,
        cotangent,
        token_valid,
        image_real,
        w_qkv,
        q_bias,
        v_bias,
        w_out,
        out_bias,
        norm1_gain,
        norm1_bias,
        scale1,
        norm2_gain,
        norm2_bias,
        w_up,
        up_bias,
        w_down,
        down_bias,
        scale2,
    ):
        images, tok_dev, width = inputs.shape
        dl = q_bias.shape[0]
        ups = up_bias.shape[0] // dl
        ff = ups * width
        shard_pos = lax.axis_index("shard")
        seq_pos = lax.axis_index("seq")
        core = shard_pos % 2
        turn_out = seq_pos // 2
        turn_in = seq_pos % 2
        pad = SPAN - tok_dev
        rows = 2 * SPAN

        def bring(array):
            got = [
                lax.ppermute(
                    lax.dynamic_index_in_dim(array, (turn + turn_out) % 2, 0, keepdims=False),
                    axes,
                    there[turn],
                )
                for turn in range(2)
            ]
            first = jnp.where(turn_in == 0, got[0], got[1])
            second = jnp.where(turn_in == 0, got[1], got[0])
            both = jnp.stack([first, second])
            return jnp.pad(both, ((0, 0), (0, pad), (0, 0))).reshape(rows, array.shape[-1])

        def give(array):
            parts = array.reshape(2, SPAN, array.shape[-1])[:, :tok_dev]
            got = [
                lax.ppermute(
                    lax.dynamic_index_in_dim(parts, (turn + seq_pos) % 2, 0, keepdims=False),
                    axes,
                    back[turn],
                )
                for turn in range(2)
            ]
            first = jnp.where(turn_out == 0, got[0], got[1])
            second = jnp.where(turn_out == 0, got[1], got[0])
            return jnp.stack([first, second])

        def exchange(array):
            return lax.ppermute(array, axes, swap)

        halves = dl % (2 * HEAD_DIM) == 0

        def interleave(own, other, part, axis, order=None):
            own = jnp.split(own, own.shape[axis] // part, axis)
            other = jnp.split(other, len(own), axis)
            blocks = []
            for idx in order or range(len(own)):
                mine, his = own[idx], other[idx]
                blocks.append(jnp.where(core == 0, mine, his))
                blocks.append(jnp.where(core == 0, his, mine))
            return jnp.concatenate(blocks, axis)

        def scatter(array, part, axis, order=None):
            if halves:
                return lax.psum_scatter(
                    array, "shard", scatter_dimension=0, axis_index_groups=chips, tiled=True
                )
            array = interleave(array, jnp.zeros_like(array), part, axis, order)
            return lax.psum_scatter(array, "shard", scatter_dimension=0, tiled=True)

        def z_reduce(array):
            split = (n_seq, array.shape[0] // n_seq, array.shape[1])
            got = lax.all_to_all(array.reshape(split), "seq", 0, 0, tiled=True)
            total = jnp.sum(got.astype(F32), axis=0).astype(BF16)
            got = lax.all_to_all(
                jnp.broadcast_to(total[None], split), "seq", 0, 0, tiled=True
            )
            return got.reshape(array.shape)

        def spread(array, part, order=None):
            if not halves:
                return array
            array = array.reshape(2, dl, array.shape[1])
            keep = lax.dynamic_index_in_dim(array, core, 0, keepdims=False)
            away = lax.dynamic_index_in_dim(array, 1 - core, 0, keepdims=False)
            return interleave(keep, exchange(away), part, 1, order)

        lengths = jnp.sum(token_valid, axis=1) * image_real
        sizes = jnp.stack([lengths // 64, lengths % 64], axis=1).reshape(1, 2 * images)
        sizes = jnp.pad(sizes.astype(BF16), ((0, 0), (0, dl - 2 * images)))
        small = jnp.concatenate(
            [
                jnp.stack(
                    [
                        q_bias,
                        v_bias,
                        out_bias,
                        norm1_gain,
                        norm1_bias,
                        scale1,
                        norm2_gain,
                        norm2_bias,
                        down_bias,
                        scale2,
                    ]
                ),
                up_bias.reshape(ups, dl),
                sizes,
            ],
            axis=0,
        )
        vecs = lax.all_gather(small, "shard", axis=1, tiled=True).astype(F32)
        qbias, vbias, obias, gain1, shift1, layer1, gain2, shift2, dbias, layer2 = (
            vecs[i] for i in range(10)
        )
        ubias = (
            vecs[10 : 10 + ups].reshape(ups, n_shard, dl).transpose(1, 0, 2).reshape(ff)
        )
        tails = vecs[10 + ups].reshape(n_shard, dl)[:, : 2 * images].reshape(n_shard, images, 2)
        all_len = tails[:, :, 0] * 64.0 + tails[:, :, 1]
        count = jnp.sum(all_len)
        my_len = all_len.reshape(-1)[
            (shard_pos // 2 * 2 + seq_pos // 2) * images + seq_pos % 2
        ]

        slot = jnp.arange(rows)
        offset = slot % SPAN

        def live_of(which):
            token = (which + 2 * (slot // SPAN)) * tok_dev + offset
            return (offset < tok_dev) & (token.astype(F32) < my_len)

        live = live_of(core)
        live_all = jnp.concatenate([live, live_of(1 - core)])
        key_bias = jnp.where(live_all, 0.0, DEAD).astype(F32)
        live = live[:, None]

        qkv_mat = lax.all_gather(w_qkv, "shard", axis=0, tiled=True)
        out_mat = lax.all_to_all(
            jnp.broadcast_to(w_out[None], (n_shard, dl, width)), "shard", 0, 0, tiled=True
        ).reshape(width, width)
        up_mat = lax.all_gather(w_up, "shard", axis=0, tiled=True)
        down_mat = lax.all_gather(w_down, "shard", axis=0, tiled=True)

        unit = 2 * HEAD_DIM
        ff_unit = max(ff // n_shard, 4 * unit)
        core_arr = core.astype(jnp.int32).reshape(1)
        x_rows = bring(inputs).astype(F32)
        normed1 = (norm_parts(x_rows)[0] * gain1 + shift1).astype(BF16)
        normed1_rec = exchange(normed1)
        qkv_bias = jnp.concatenate([qbias, jnp.zeros_like(qbias), vbias])
        scale = jnp.concatenate(
            [jnp.full((width,), HEAD_DIM ** (-0.5), BF16), jnp.ones((2 * width,), BF16)]
        )
        qkv = (jnp.dot(normed1, qkv_mat, preferred_element_type=F32) + qkv_bias).astype(BF16) * scale
        rec = exchange(pick_other(core_arr, qkv, unit))
        mixed_mine, lse = attention(core_arr, qkv, rec, key_bias)
        both = bring(jnp.concatenate([teacher, cotangent], axis=-1))
        teach_rows = both[:, :width].astype(F32)
        cot_rows = both[:, width:].astype(F32)
        mixed = merge(core_arr, (mixed_mine,), (exchange(mixed_mine[rows:]),), rows, unit, 1)
        attn_out = jnp.dot(mixed, out_mat, preferred_element_type=F32) + obias
        resid1 = x_rows + layer1 * attn_out
        normed2 = (norm_parts(resid1)[0] * gain2 + shift2).astype(BF16)
        normed2_rec = exchange(normed2)
        pre = jnp.dot(normed2, up_mat, preferred_element_type=F32) + ubias
        act = (pre * gelu_parts(pre)[0]).astype(BF16)
        act_rec = exchange(act)
        branch = jnp.dot(act, down_mat, preferred_element_type=F32) + dbias
        resid2 = resid1 + layer2 * branch
        out_rows = jnp.where(live, resid2, x_rows)
        diff = jnp.where(live, out_rows - teach_rows, 0.0)
        err = jnp.sum(diff * diff)
        result = give(out_rows.astype(BF16))

        g_out = cot_rows + 2.0 * diff / (count * width)
        g_keep = jnp.where(live, g_out, 0.0)
        g_pass = g_out - g_keep
        d_scale2 = jnp.sum(g_keep * branch, axis=0)
        g_branch = (g_keep * layer2).astype(BF16)
        d_down_bias = jnp.sum(g_branch.astype(F32), axis=0)
        g_branch_rec = exchange(g_branch)

        tile = 2 * unit
        whole = pl.BlockSpec((rows, width), lambda i, core: (0, 0))
        strip = pl.BlockSpec((rows, tile), lambda i, core: (0, i))
        per = ff_unit // tile
        act_spec = pl.BlockSpec(
            (rows, tile), lambda i, core: (0, (2 * (i // per) + core[0]) * per + i % per)
        )
        w_down_part = weight_grad(
            core_arr,
            (act, act_rec, g_branch, g_branch_rec),
            [act_spec, act_spec, whole, whole],
            (ff // 2, width),
            tile,
        )
        p_down = scatter(w_down_part, ff_unit, 0)
        g_hidden = jnp.einsum("rd,fd->rf", g_branch, down_mat, preferred_element_type=F32)
        phi_sum, phi = gelu_parts(pre)
        g_pre = (g_hidden * (phi_sum + pre * phi)).astype(BF16)
        d_up_bias = jnp.sum(g_pre.astype(F32), axis=0)
        g_pre_rec = exchange(g_pre)
        n_units = ff // ff_unit // 2
        w_up_part = weight_grad(
            core_arr,
            (normed2, normed2_rec) + (g_pre,) * n_units + (g_pre_rec,) * n_units,
            [strip, strip]
            + [
                pl.BlockSpec((rows, ff_unit), lambda i, core, j=j: (0, 2 * j + core[0]))
                for j in range(n_units)
            ]
            * 2,
            (width, ff // 2),
            tile,
        )
        p_up = scatter(w_up_part, ff_unit, 1)
        g_norm2 = jnp.einsum("rf,df->rd", g_pre, up_mat, preferred_element_type=F32)
        g_ln2, d_gain2, d_shift2 = norm_back(resid1, gain2, g_norm2)
        g_resid1 = g_keep + g_ln2
        d_scale1 = jnp.sum(g_resid1 * attn_out, axis=0)
        g_attn = (g_resid1 * layer1).astype(BF16)
        d_out_bias = jnp.sum(g_attn.astype(F32), axis=0)
        g_attn_rec = exchange(g_attn)
        out_mine = lax.dynamic_index_in_dim(
            out_mat.reshape(width // unit // 2, 2, unit, width), core, 1, keepdims=False
        ).reshape(width // 2, width)

        def mixed_grad(array):
            return jnp.einsum("rd,cd->rc", array, out_mine, preferred_element_type=F32).astype(BF16)

        w_out_part = weight_grad(
            core_arr,
            (mixed_mine, mixed_mine, g_attn, g_attn_rec),
            [strip, pl.BlockSpec((rows, tile), lambda i, core: (1, i)), whole, whole],
            (width // 2, width),
            tile,
        )
        p_out = scatter(w_out_part, unit, 0)
        g_mine = (mixed_grad(g_attn), mixed_grad(g_attn_rec))
        pairs = width // 2 // unit
        g_alls = [
            attention_back(
                core_arr, qkv, rec, *g_mine, mixed_mine, lse, key_bias, first, first + pairs // 2
            )
            for first in (0, pairs // 2)
        ]
        g_recs = [exchange(part[rows:]) for part in g_alls]
        order = [
            pair // 2 * 6 + part * 2 + pair % 2 for part in range(3) for pair in range(pairs)
        ]
        half_cols = 3 * width // 4
        w_qkv_part = weight_grad(
            core_arr,
            (normed1, normed1_rec) + tuple(g_alls) * 2,
            [strip, strip]
            + [pl.BlockSpec((rows, half_cols), lambda i, core: (0, 0))] * 2
            + [pl.BlockSpec((rows, half_cols), lambda i, core: (1, 0))] * 2,
            (width, 3 * width // 2),
            tile,
        )
        p_qkv = scatter(w_qkv_part, unit, 1, order)
        g_qkv = merge(core_arr, g_alls, g_recs, rows, unit, 3)
        d_qkv_bias = jnp.sum(g_qkv.astype(F32), axis=0)
        g_norm1 = jnp.einsum("re,de->rd", g_qkv, qkv_mat, preferred_element_type=F32)
        g_ln1, d_gain1, d_shift1 = norm_back(x_rows, gain1, g_norm1)
        g_in = give((g_pass + g_resid1 + g_ln1).astype(BF16)).astype(F32)

        p_down = z_reduce(p_down)
        p_up = z_reduce(p_up)
        p_out, p_qkv = lax.psum((p_out, p_qkv), "seq")
        p_up = spread(p_up, ff_unit)
        p_qkv = spread(p_qkv, unit, order)
        sums = jnp.concatenate(
            [
                jnp.stack(
                    [
                        d_qkv_bias[:width],
                        d_qkv_bias[2 * width :],
                        d_out_bias,
                        d_gain1,
                        d_shift1,
                        d_scale1,
                        d_gain2,
                        d_shift2,
                        d_down_bias,
                        d_scale2,
                    ]
                ),
                d_up_bias.reshape(n_shard, ups, dl).transpose(1, 0, 2).reshape(ups, width),
                jnp.full((1, width), err),
            ],
            axis=0,
        )
        kinds = sums.shape[0]
        sums = sums.reshape(kinds, n_shard, 1, dl).transpose(1, 2, 0, 3)
        sums = jnp.broadcast_to(sums, (n_shard, n_seq, kinds, dl))
        sums = lax.all_to_all(
            sums.reshape(n_shard * n_seq, kinds, dl), axes, 0, 0, tiled=True
        )
        mine = jnp.sum(sums, axis=0)
        loss = mine[10 + ups, 0] / (count * width)
        (
            s_qb, s_vb, s_ob, s_g1, s_b1, s_l1, s_g2, s_b2, s_db, s_l2
        ) = (mine[i] for i in range(10))
        s_ub = mine[10 : 10 + ups].reshape(ups * dl)
        return (
            result,
            loss,
            g_in,
            p_qkv.astype(F32),
            s_qb,
            s_vb,
            p_out.astype(F32),
            s_ob,
            s_g1,
            s_b1,
            s_l1,
            s_g2,
            s_b2,
            p_up.astype(F32),
            s_ub,
            p_down.astype(F32),
            s_db,
            s_l2,
        )

    return inner


def solution(mesh):
    tokens = P("shard", "seq", None)
    matrix = P("shard", None)
    vector = P("shard")
    in_specs = (
        tokens,
        tokens,
        tokens,
        matrix,
        vector,
        matrix,
        vector,
        vector,
        matrix,
        vector,
        vector,
        vector,
        vector,
        vector,
        vector,
        matrix,
        vector,
        matrix,
        vector,
        vector,
    )
    out_specs = (
        tokens,
        P(),
        tokens,
        matrix,
        vector,
        vector,
        matrix,
        vector,
        vector,
        vector,
        vector,
        vector,
        vector,
        matrix,
        vector,
        matrix,
        vector,
        vector,
    )
    return jax.shard_map(
        make_step(mesh.shape["shard"], mesh.shape["seq"]),
        mesh=mesh,
        in_specs=in_specs,
        out_specs=out_specs,
        check_vma=False,
    )
```

```python
import functools

import jax
import jax.numpy as jnp
from jax import lax
from jax.experimental import pallas as pl
from jax.experimental.pallas import tpu as pltpu
from jax.sharding import PartitionSpec as P

HEAD_DIM = 64
DEAD = -1000000000.0
SPAN = 352
F32 = jnp.float32
BF16 = jnp.bfloat16
NT = (((1,), (1,)), ((), ()))
TN = (((0,), (0,)), ((), ()))


def lane_masks(dtype):
    lane = lax.broadcasted_iota(jnp.int32, (1, 2 * HEAD_DIM), 1)
    low = jnp.where(lane < HEAD_DIM, 1.0, 0.0).astype(F32)
    return low.astype(dtype), (1.0 - low).astype(dtype)


def forward_kernel(
    core_ref, q_own, k_own, v_own, q_rec, k_rec, v_rec, bias_ref, o_ref, lse_ref, q_s, k_s, v_s, lse_s
):
    half = q_own.shape[0]
    for all_ref, own, rec in ((q_s, q_own, q_rec), (k_s, k_own, k_rec), (v_s, v_own, v_rec)):
        all_ref[:half, :] = own[...]
        all_ref[half:, :] = rec[...]
    masks = lane_masks(BF16)
    low, high = lane_masks(F32)
    bias = bias_ref[...]

    def block(idx, carry):
        row = pl.multiple_of(idx * SPAN, 16)
        query = q_s[pl.ds(row, SPAN), :]
        outs = []
        sums = []
        for mask in masks:
            scores = lax.dot_general(query * mask, k_s[...], NT, preferred_element_type=F32) + bias
            peak = jnp.max(scores, axis=-1, keepdims=True)
            weight = jnp.exp(scores - peak)
            total = jnp.sum(weight, axis=-1, keepdims=True)
            mixed = jnp.dot(weight.astype(BF16), v_s[...], preferred_element_type=F32)
            outs.append(mixed / total)
            sums.append(peak + jnp.log(total))
        o_ref[pl.ds(row, SPAN), :] = (outs[0] * low + outs[1] * high).astype(BF16)
        lse_s[pl.ds(row, SPAN), :] = sums[0] * low + sums[1] * high
        return carry

    lax.fori_loop(0, 2 * half // SPAN, block, 0)
    turned = jnp.transpose(lse_s[...])
    lse_ref[0, 0:8, :] = turned[0:8, :]
    lse_ref[0, 8:16, :] = turned[HEAD_DIM : HEAD_DIM + 8, :]


def backward_kernel(
    core_ref,
    q_own,
    k_own,
    v_own,
    q_rec,
    k_rec,
    v_rec,
    g_own,
    g_rec,
    o_ref,
    lse_ref,
    bias_ref,
    d_ref,
    q_s,
    k_s,
    v_s,
    g_s,
    dqt_s,
):
    half = q_own.shape[0]
    width = d_ref.shape[1] // 3
    pair = pl.program_id(0)
    cols = [pl.multiple_of(part * width + pair * 2 * HEAD_DIM, 128) for part in range(3)]
    low, high = lane_masks(BF16)
    for all_ref, own, rec in ((k_s, k_own, k_rec), (v_s, v_own, v_rec)):
        all_ref[:half, :] = own[...]
        all_ref[half:, :] = rec[...]
    for all_ref, own, rec in ((q_s, q_own, q_rec), (g_s, g_own, g_rec)):
        for head, mask in enumerate((low, high)):
            all_ref[head, :half, :] = own[...] * mask
            all_ref[head, half:, :] = rec[...] * mask
    dots_own = jnp.transpose(g_own[...].astype(F32) * o_ref[:half, :].astype(F32))
    dots_rec = jnp.transpose(g_rec[...].astype(F32) * o_ref[half:, :].astype(F32))
    dots = jnp.concatenate([dots_own, dots_rec], axis=1)
    inner = (
        jnp.sum(dots[:HEAD_DIM], axis=0, keepdims=True),
        jnp.sum(dots[HEAD_DIM:], axis=0, keepdims=True),
    )
    dqt_s[...] = jnp.zeros_like(dqt_s)

    def block(idx, carry):
        row = pl.multiple_of(idx * SPAN, 16)
        key = k_s[pl.ds(row, SPAN), :]
        value = v_s[pl.ds(row, SPAN), :]
        bias = bias_ref[pl.ds(row, SPAN), :]
        key_t = jnp.transpose(key.astype(F32)).astype(BF16)
        dk = jnp.zeros((SPAN, 2 * HEAD_DIM), F32)
        dv = jnp.zeros((SPAN, 2 * HEAD_DIM), F32)
        for head in range(2):
            query = q_s[head]
            grad = g_s[head]
            lse = lse_ref[0, 8 * head : 8 * head + 1, :]
            prob = jnp.exp(
                lax.dot_general(key, query, NT, preferred_element_type=F32) + bias - lse
            )
            g_prob = lax.dot_general(value, grad, NT, preferred_element_type=F32)
            g_score = (prob * (g_prob - inner[head])).astype(BF16)
            dv = dv + jnp.dot(prob.astype(BF16), grad, preferred_element_type=F32)
            dk = dk + jnp.dot(g_score, query, preferred_element_type=F32)
            rows = slice(HEAD_DIM * head, HEAD_DIM * (head + 1))
            dqt_s[rows, :] += jnp.dot(key_t[rows, :], g_score, preferred_element_type=F32)
        d_ref[pl.ds(row, SPAN), pl.ds(cols[1], 2 * HEAD_DIM)] = dk.astype(BF16)
        d_ref[pl.ds(row, SPAN), pl.ds(cols[2], 2 * HEAD_DIM)] = dv.astype(BF16)
        return carry

    lax.fori_loop(0, 2 * half // SPAN, block, 0)
    dq = (jnp.transpose(dqt_s[...]) * HEAD_DIM ** (-0.5)).astype(BF16)
    d_ref[:, pl.ds(cols[0], 2 * HEAD_DIM)] = dq


def call(kernel, core, args, grid, in_specs, out_specs, out_shape, scratch, flops, trans):
    moved = sum(arg.size * arg.dtype.itemsize for arg in args)
    return pl.pallas_call(
        kernel,
        grid_spec=pltpu.PrefetchScalarGridSpec(
            num_scalar_prefetch=1,
            grid=grid,
            in_specs=in_specs,
            out_specs=out_specs,
            scratch_shapes=scratch,
        ),
        out_shape=out_shape,
        cost_estimate=pl.CostEstimate(flops=flops, transcendentals=trans, bytes_accessed=moved),
        compiler_params=pltpu.CompilerParams(vmem_limit_bytes=56 * 1024 * 1024),
    )(core, *args)


def head_blocks(half, pairs, first=0):
    wide = 2 * HEAD_DIM
    own = [
        pl.BlockSpec(
            (half, wide),
            lambda pair, core, part=part: (0, 2 * (part * pairs + pair + first) + core[0]),
        )
        for part in range(3)
    ]
    rec = [
        pl.BlockSpec((half, wide), lambda pair, core, part=part: (0, part * pairs + pair + first))
        for part in range(3)
    ]
    return own + rec


def attention(core, qkv, rec, bias):
    half = rec.shape[0]
    width = rec.shape[1] // 3
    wide = 2 * HEAD_DIM
    pairs = width // wide
    full = 2 * half
    ops = pairs * 2 * full * full
    return call(
        forward_kernel,
        core,
        (qkv, qkv, qkv, rec, rec, rec, bias.reshape(1, full)),
        (pairs,),
        head_blocks(half, pairs) + [pl.BlockSpec((1, full), lambda pair, core: (0, 0))],
        [
            pl.BlockSpec((full, wide), lambda pair, core: (0, pair)),
            pl.BlockSpec((1, 16, full), lambda pair, core: (pair, 0, 0)),
        ],
        [
            jax.ShapeDtypeStruct((full, width), BF16),
            jax.ShapeDtypeStruct((pairs, 16, full), F32),
        ],
        [pltpu.VMEM((full, wide), BF16)] * 3 + [pltpu.VMEM((full, wide), F32)],
        ops * 4 * 256,
        ops,
    )


def attention_back(core, qkv, rec, g_own, g_rec, mixed, lse, bias, first, last):
    half = rec.shape[0]
    wide = 2 * HEAD_DIM
    pairs = rec.shape[1] // 3 // wide
    here = last - first
    full = 2 * half
    col = pl.BlockSpec((half, wide), lambda pair, core: (0, pair + first))
    ops = here * 2 * full * full
    return call(
        backward_kernel,
        core,
        (qkv, qkv, qkv, rec, rec, rec, g_own, g_rec, mixed, lse, bias.reshape(full, 1)),
        (here,),
        head_blocks(half, pairs, first)
        + [
            col,
            col,
            pl.BlockSpec((full, wide), lambda pair, core: (0, pair + first)),
            pl.BlockSpec((1, 16, full), lambda pair, core: (pair + first, 0, 0)),
            pl.BlockSpec((full, 1), lambda pair, core: (0, 0)),
        ],
        pl.BlockSpec((full, 3 * here * wide), lambda pair, core: (0, 0)),
        jax.ShapeDtypeStruct((full, 3 * here * wide), BF16),
        [
            pltpu.VMEM((2, full, wide), BF16),
            pltpu.VMEM((full, wide), BF16),
            pltpu.VMEM((full, wide), BF16),
            pltpu.VMEM((2, full, wide), BF16),
            pltpu.VMEM((wide, full), F32),
        ],
        ops * 10 * 256,
        ops,
    )


def grad_kernel(core_ref, a_own, a_rec, *refs):
    out = refs[-1]
    count = len(refs) // 2
    start = 0
    for b_own, b_rec in zip(refs[:count], refs[count:-1]):
        total = lax.dot_general(a_own[...], b_own[...], TN, preferred_element_type=F32)
        total += lax.dot_general(a_rec[...], b_rec[...], TN, preferred_element_type=F32)
        out[:, start : start + b_own.shape[1]] = total.astype(BF16)
        start += b_own.shape[1]


def weight_grad(core, args, specs, shape, tile):
    rows = 4 * SPAN
    return call(
        grad_kernel,
        core,
        args,
        (shape[0] // tile,),
        specs,
        pl.BlockSpec((tile, shape[1]), lambda i, core: (i, 0)),
        jax.ShapeDtypeStruct(shape, BF16),
        [],
        2 * rows * shape[0] * shape[1],
        0,
    )


def pick_kernel(unit, core_ref, src, dst):
    for parity in range(2):

        @pl.when(core_ref[0] == parity)
        def _():
            for idx in range(dst.shape[1] // unit):
                low = (2 * idx + 1 - parity) * unit
                dst[:, idx * unit : (idx + 1) * unit] = src[:, low : low + unit]


def pick_other(core, array, unit):
    rows, width = array.shape
    wide = 1024
    return call(
        functools.partial(pick_kernel, unit),
        core,
        (array,),
        (width // wide,),
        [pl.BlockSpec((rows, wide), lambda i, core: (0, i))],
        pl.BlockSpec((rows, wide // 2), lambda i, core: (0, i)),
        jax.ShapeDtypeStruct((rows, width // 2), array.dtype),
        [],
        0,
        0,
    )


def merge_kernel(unit, core_ref, *refs):
    dst = refs[-1]
    count = len(refs) // 2
    for parity in range(2):

        @pl.when(core_ref[0] == parity)
        def _():
            at = 0
            for own, rec in zip(refs[:count], refs[count:-1]):
                for idx in range(own.shape[1] // unit):
                    cols = slice(idx * unit, (idx + 1) * unit)
                    for side, src in enumerate((own, rec)):
                        low = at + (parity + side) % 2 * unit
                        dst[:, low : low + unit] = src[:, cols]
                    at += 2 * unit


def merge(core, owns, recs, rows, unit, steps):
    width = sum(rec.shape[1] for rec in recs)
    specs = [pl.BlockSpec((rows, rec.shape[1] // steps), lambda i, core: (0, i)) for rec in recs]
    return call(
        functools.partial(merge_kernel, unit),
        core,
        tuple(owns) + tuple(recs),
        (steps,),
        specs + specs,
        pl.BlockSpec((rows, 2 * width // steps), lambda i, core: (0, i)),
        jax.ShapeDtypeStruct((rows, 2 * width), recs[0].dtype),
        [],
        0,
        0,
    )


def gelu_parts(values):
    phi_sum = 0.5 * (1.0 + lax.erf(values * 0.7071067811865476))
    phi = jnp.exp(-0.5 * values * values) * 0.3989422804014327
    return phi_sum, phi


def norm_parts(values):
    center = values - jnp.mean(values, axis=-1, keepdims=True)
    spread = jnp.mean(center * center, axis=-1, keepdims=True)
    scale = lax.rsqrt(spread + 1e-06)
    return center * scale, scale


def norm_back(values, gain, grad):
    unit, scale = norm_parts(values)
    scaled = grad * gain
    drift = jnp.mean(scaled, axis=-1, keepdims=True)
    slope = jnp.mean(scaled * unit, axis=-1, keepdims=True)
    back = scale * (scaled - drift - unit * slope)
    return back, jnp.sum(grad * unit, axis=0), jnp.sum(grad, axis=0)


def make_step(n_shard, n_seq):
    def place(shard, seq):
        return shard * n_seq + seq

    def route(turn):
        moves = []
        for shard in range(n_shard):
            for seq in range(n_seq):
                src = place(shard, seq)
                dst = place(
                    shard // 2 * 2 + seq % 2, 2 * (shard % 2) + (turn + seq // 2) % 2
                )
                if src != dst:
                    moves.append((src, dst))
        return moves

    there = (route(0), route(1))
    back = tuple([(dst, src) for src, dst in moves] for moves in there)
    swap = [
        (place(shard, seq), place(shard ^ 1, seq))
        for shard in range(n_shard)
        for seq in range(n_seq)
    ]
    axes = ("shard", "seq")
    chips = [list(range(core, n_shard, 2)) for core in range(2)]

    def inner(
        inputs,
        teacher,
        cotangent,
        token_valid,
        image_real,
        w_qkv,
        q_bias,
        v_bias,
        w_out,
        out_bias,
        norm1_gain,
        norm1_bias,
        scale1,
        norm2_gain,
        norm2_bias,
        w_up,
        up_bias,
        w_down,
        down_bias,
        scale2,
    ):
        images, tok_dev, width = inputs.shape
        dl = q_bias.shape[0]
        ups = up_bias.shape[0] // dl
        ff = ups * width
        shard_pos = lax.axis_index("shard")
        seq_pos = lax.axis_index("seq")
        core = shard_pos % 2
        turn_out = seq_pos // 2
        turn_in = seq_pos % 2
        pad = SPAN - tok_dev
        rows = 2 * SPAN

        def move(array, turn, moves):
            stays = (core == turn_in) & (seq_pos == 2 * core + (turn + turn_out) % 2)
            return jnp.where(stays, array, lax.ppermute(array, axes, moves))

        def bring(array):
            got = [
                move(
                    lax.dynamic_index_in_dim(array, (turn + turn_out) % 2, 0, keepdims=False),
                    turn,
                    there[turn],
                )
                for turn in range(2)
            ]
            first = jnp.where(turn_in == 0, got[0], got[1])
            second = jnp.where(turn_in == 0, got[1], got[0])
            both = jnp.stack([first, second])
            return jnp.pad(both, ((0, 0), (0, pad), (0, 0))).reshape(rows, array.shape[-1])

        def give(array):
            parts = array.reshape(2, SPAN, array.shape[-1])[:, :tok_dev]
            got = [
                move(
                    lax.dynamic_index_in_dim(parts, (turn + seq_pos) % 2, 0, keepdims=False),
                    turn,
                    back[turn],
                )
                for turn in range(2)
            ]
            first = jnp.where(turn_out == 0, got[0], got[1])
            second = jnp.where(turn_out == 0, got[1], got[0])
            return jnp.stack([first, second])

        def exchange(array):
            return lax.ppermute(array, axes, swap)

        halves = dl % (2 * HEAD_DIM) == 0

        def interleave(own, other, part, axis, order=None):
            own = jnp.split(own, own.shape[axis] // part, axis)
            other = jnp.split(other, len(own), axis)
            blocks = []
            for idx in order or range(len(own)):
                mine, his = own[idx], other[idx]
                blocks.append(jnp.where(core == 0, mine, his))
                blocks.append(jnp.where(core == 0, his, mine))
            return jnp.concatenate(blocks, axis)

        def scatter(array, part, axis, order=None):
            if halves:
                return lax.psum_scatter(
                    array, "shard", scatter_dimension=0, axis_index_groups=chips, tiled=True
                )
            array = interleave(array, jnp.zeros_like(array), part, axis, order)
            return lax.psum_scatter(array, "shard", scatter_dimension=0, tiled=True)

        def z_reduce(array):
            split = (n_seq, array.shape[0] // n_seq, array.shape[1])
            got = lax.all_to_all(array.reshape(split), "seq", 0, 0, tiled=True)
            total = jnp.sum(got.astype(F32), axis=0).astype(BF16)
            got = lax.all_to_all(
                jnp.broadcast_to(total[None], split), "seq", 0, 0, tiled=True
            )
            return got.reshape(array.shape)

        def spread(array, part, order=None):
            if not halves:
                return array
            array = array.reshape(2, dl, array.shape[1])
            keep = lax.dynamic_index_in_dim(array, core, 0, keepdims=False)
            away = lax.dynamic_index_in_dim(array, 1 - core, 0, keepdims=False)
            return interleave(keep, exchange(away), part, 1, order)

        lengths = jnp.sum(token_valid, axis=1) * image_real
        sizes = jnp.stack([lengths // 64, lengths % 64], axis=1).reshape(1, 2 * images)
        sizes = jnp.pad(sizes.astype(BF16), ((0, 0), (0, dl - 2 * images)))
        small = jnp.concatenate(
            [
                jnp.stack(
                    [
                        q_bias,
                        v_bias,
                        out_bias,
                        norm1_gain,
                        norm1_bias,
                        scale1,
                        norm2_gain,
                        norm2_bias,
                        down_bias,
                        scale2,
                    ]
                ),
                up_bias.reshape(ups, dl),
                sizes,
            ],
            axis=0,
        )
        vecs = lax.all_gather(small, "shard", axis=1, tiled=True).astype(F32)
        qbias, vbias, obias, gain1, shift1, layer1, gain2, shift2, dbias, layer2 = (
            vecs[i] for i in range(10)
        )
        ubias = (
            vecs[10 : 10 + ups].reshape(ups, n_shard, dl).transpose(1, 0, 2).reshape(ff)
        )
        tails = vecs[10 + ups].reshape(n_shard, dl)[:, : 2 * images].reshape(n_shard, images, 2)
        all_len = tails[:, :, 0] * 64.0 + tails[:, :, 1]
        count = jnp.sum(all_len)
        my_len = all_len.reshape(-1)[
            (shard_pos // 2 * 2 + seq_pos // 2) * images + seq_pos % 2
        ]

        slot = jnp.arange(rows)
        offset = slot % SPAN

        def live_of(which):
            token = (which + 2 * (slot // SPAN)) * tok_dev + offset
            return (offset < tok_dev) & (token.astype(F32) < my_len)

        live = live_of(core)
        live_all = jnp.concatenate([live, live_of(1 - core)])
        key_bias = jnp.where(live_all, 0.0, DEAD).astype(F32)
        live = live[:, None]

        qkv_mat = lax.all_gather(w_qkv, "shard", axis=0, tiled=True)
        out_own = lax.all_to_all(
            jnp.broadcast_to(w_out[None], (n_shard // 2, dl, width)),
            "shard",
            0,
            0,
            axis_index_groups=chips,
            tiled=True,
        )
        out_rec = exchange(out_own)
        out_mat = jnp.stack(
            [jnp.where(core == 0, out_own, out_rec), jnp.where(core == 0, out_rec, out_own)], axis=1
        ).reshape(width, width)
        up_mat = lax.all_gather(w_up, "shard", axis=0, tiled=True)
        down_mat = lax.all_gather(w_down, "shard", axis=0, tiled=True)

        unit = 2 * HEAD_DIM
        ff_unit = max(ff // n_shard, 4 * unit)
        core_arr = core.astype(jnp.int32).reshape(1)
        x_rows = bring(inputs).astype(F32)
        normed1 = (norm_parts(x_rows)[0] * gain1 + shift1).astype(BF16)
        normed1_rec = exchange(normed1)
        qkv_bias = jnp.concatenate([qbias, jnp.zeros_like(qbias), vbias])
        scale = jnp.concatenate(
            [jnp.full((width,), HEAD_DIM ** (-0.5), BF16), jnp.ones((2 * width,), BF16)]
        )
        qkv = (jnp.dot(normed1, qkv_mat, preferred_element_type=F32) + qkv_bias).astype(BF16) * scale
        rec = exchange(pick_other(core_arr, qkv, unit))
        mixed_mine, lse = attention(core_arr, qkv, rec, key_bias)
        both = bring(jnp.concatenate([teacher, cotangent], axis=-1))
        teach_rows = both[:, :width].astype(F32)
        cot_rows = both[:, width:].astype(F32)
        mixed = merge(core_arr, (mixed_mine,), (exchange(mixed_mine[rows:]),), rows, unit, 1)
        attn_out = jnp.dot(mixed, out_mat, preferred_element_type=F32) + obias
        resid1 = x_rows + layer1 * attn_out
        normed2 = (norm_parts(resid1)[0] * gain2 + shift2).astype(BF16)
        normed2_rec = exchange(normed2)
        pre = jnp.dot(normed2, up_mat, preferred_element_type=F32) + ubias
        act = (pre * gelu_parts(pre)[0]).astype(BF16)
        act_rec = exchange(act)
        branch = jnp.dot(act, down_mat, preferred_element_type=F32) + dbias
        resid2 = resid1 + layer2 * branch
        out_rows = jnp.where(live, resid2, x_rows)
        diff = jnp.where(live, out_rows - teach_rows, 0.0)
        err = jnp.sum(diff * diff)
        result = give(out_rows.astype(BF16))

        g_out = cot_rows + 2.0 * diff / (count * width)
        g_keep = jnp.where(live, g_out, 0.0)
        g_pass = g_out - g_keep
        d_scale2 = jnp.sum(g_keep * branch, axis=0)
        g_branch = (g_keep * layer2).astype(BF16)
        d_down_bias = jnp.sum(g_branch.astype(F32), axis=0)
        g_branch_rec = exchange(g_branch)

        tile = 2 * unit
        whole = pl.BlockSpec((rows, width), lambda i, core: (0, 0))
        strip = pl.BlockSpec((rows, tile), lambda i, core: (0, i))
        per = ff_unit // tile
        act_spec = pl.BlockSpec(
            (rows, tile), lambda i, core: (0, (2 * (i // per) + core[0]) * per + i % per)
        )
        w_down_part = weight_grad(
            core_arr,
            (act, act_rec, g_branch, g_branch_rec),
            [act_spec, act_spec, whole, whole],
            (ff // 2, width),
            tile,
        )
        p_down = scatter(w_down_part, ff_unit, 0)
        g_hidden = jnp.einsum("rd,fd->rf", g_branch, down_mat, preferred_element_type=F32)
        phi_sum, phi = gelu_parts(pre)
        g_pre = (g_hidden * (phi_sum + pre * phi)).astype(BF16)
        d_up_bias = jnp.sum(g_pre.astype(F32), axis=0)
        g_pre_rec = exchange(g_pre)
        n_units = ff // ff_unit // 2
        w_up_part = weight_grad(
            core_arr,
            (normed2, normed2_rec) + (g_pre,) * n_units + (g_pre_rec,) * n_units,
            [strip, strip]
            + [
                pl.BlockSpec((rows, ff_unit), lambda i, core, j=j: (0, 2 * j + core[0]))
                for j in range(n_units)
            ]
            * 2,
            (width, ff // 2),
            tile,
        )
        p_up = scatter(w_up_part, ff_unit, 1)
        g_norm2 = jnp.einsum("rf,df->rd", g_pre, up_mat, preferred_element_type=F32)
        g_ln2, d_gain2, d_shift2 = norm_back(resid1, gain2, g_norm2)
        g_resid1 = g_keep + g_ln2
        d_scale1 = jnp.sum(g_resid1 * attn_out, axis=0)
        g_attn = (g_resid1 * layer1).astype(BF16)
        d_out_bias = jnp.sum(g_attn.astype(F32), axis=0)
        g_attn_rec = exchange(g_attn)
        out_mine = lax.dynamic_index_in_dim(
            out_mat.reshape(width // unit // 2, 2, unit, width), core, 1, keepdims=False
        ).reshape(width // 2, width)

        def mixed_grad(array):
            return jnp.einsum("rd,cd->rc", array, out_mine, preferred_element_type=F32).astype(BF16)

        w_out_part = weight_grad(
            core_arr,
            (mixed_mine, mixed_mine, g_attn, g_attn_rec),
            [strip, pl.BlockSpec((rows, tile), lambda i, core: (1, i)), whole, whole],
            (width // 2, width),
            tile,
        )
        p_out = scatter(w_out_part, unit, 0)
        g_mine = (mixed_grad(g_attn), mixed_grad(g_attn_rec))
        pairs = width // 2 // unit
        g_alls = [
            attention_back(
                core_arr, qkv, rec, *g_mine, mixed_mine, lse, key_bias, first, first + pairs // 2
            )
            for first in (0, pairs // 2)
        ]
        g_recs = [exchange(part[rows:]) for part in g_alls]
        order = [
            pair // 2 * 6 + part * 2 + pair % 2 for part in range(3) for pair in range(pairs)
        ]
        half_cols = 3 * width // 4
        w_qkv_part = weight_grad(
            core_arr,
            (normed1, normed1_rec) + tuple(g_alls) * 2,
            [strip, strip]
            + [pl.BlockSpec((rows, half_cols), lambda i, core: (0, 0))] * 2
            + [pl.BlockSpec((rows, half_cols), lambda i, core: (1, 0))] * 2,
            (width, 3 * width // 2),
            tile,
        )
        p_qkv = scatter(w_qkv_part, unit, 1, order)
        g_qkv = merge(core_arr, g_alls, g_recs, rows, unit, 3)
        d_qkv_bias = jnp.sum(g_qkv.astype(F32), axis=0)
        g_norm1 = jnp.einsum("re,de->rd", g_qkv, qkv_mat, preferred_element_type=F32)
        g_ln1, d_gain1, d_shift1 = norm_back(x_rows, gain1, g_norm1)
        g_in = give((g_pass + g_resid1 + g_ln1).astype(BF16)).astype(F32)

        p_down = z_reduce(p_down)
        p_up = z_reduce(p_up)
        p_out, p_qkv = lax.psum((p_out, p_qkv), "seq")
        p_up = spread(p_up, ff_unit)
        p_qkv = spread(p_qkv, unit, order)
        sums = jnp.concatenate(
            [
                jnp.stack(
                    [
                        d_qkv_bias[:width],
                        d_qkv_bias[2 * width :],
                        d_out_bias,
                        d_gain1,
                        d_shift1,
                        d_scale1,
                        d_gain2,
                        d_shift2,
                        d_down_bias,
                        d_scale2,
                    ]
                ),
                d_up_bias.reshape(n_shard, ups, dl).transpose(1, 0, 2).reshape(ups, width),
                jnp.full((1, width), err),
            ],
            axis=0,
        )
        kinds = sums.shape[0]
        sums = sums.reshape(kinds, n_shard, 1, dl).transpose(1, 2, 0, 3)
        sums = jnp.broadcast_to(sums, (n_shard, n_seq, kinds, dl))
        sums = lax.all_to_all(
            sums.reshape(n_shard * n_seq, kinds, dl), axes, 0, 0, tiled=True
        )
        mine = jnp.sum(sums, axis=0)
        loss = mine[10 + ups, 0] / (count * width)
        (
            s_qb, s_vb, s_ob, s_g1, s_b1, s_l1, s_g2, s_b2, s_db, s_l2
        ) = (mine[i] for i in range(10))
        s_ub = mine[10 : 10 + ups].reshape(ups * dl)
        return (
            result,
            loss,
            g_in,
            p_qkv.astype(F32),
            s_qb,
            s_vb,
            p_out.astype(F32),
            s_ob,
            s_g1,
            s_b1,
            s_l1,
            s_g2,
            s_b2,
            p_up.astype(F32),
            s_ub,
            p_down.astype(F32),
            s_db,
            s_l2,
        )

    return inner


def solution(mesh):
    tokens = P("shard", "seq", None)
    matrix = P("shard", None)
    vector = P("shard")
    in_specs = (
        tokens,
        tokens,
        tokens,
        matrix,
        vector,
        matrix,
        vector,
        vector,
        matrix,
        vector,
        vector,
        vector,
        vector,
        vector,
        vector,
        matrix,
        vector,
        matrix,
        vector,
        vector,
    )
    out_specs = (
        tokens,
        P(),
        tokens,
        matrix,
        vector,
        vector,
        matrix,
        vector,
        vector,
        vector,
        vector,
        vector,
        vector,
        matrix,
        vector,
        matrix,
        vector,
        vector,
    )
    return jax.shard_map(
        make_step(mesh.shape["shard"], mesh.shape["seq"]),
        mesh=mesh,
        in_specs=in_specs,
        out_specs=out_specs,
        check_vma=False,
    )
```

```python
import functools

import jax
import jax.numpy as jnp
from jax import lax
from jax.experimental import pallas as pl
from jax.experimental.pallas import tpu as pltpu
from jax.sharding import PartitionSpec as P

HEAD_DIM = 64
DEAD = -1000000000.0
SPAN = 352
F32 = jnp.float32
BF16 = jnp.bfloat16
NT = (((1,), (1,)), ((), ()))
TN = (((0,), (0,)), ((), ()))


def lane_masks(dtype):
    lane = lax.broadcasted_iota(jnp.int32, (1, 2 * HEAD_DIM), 1)
    low = jnp.where(lane < HEAD_DIM, 1.0, 0.0).astype(F32)
    return low.astype(dtype), (1.0 - low).astype(dtype)


def forward_kernel(
    core_ref, q_own, k_own, v_own, q_rec, k_rec, v_rec, bias_ref, o_ref, lse_ref, q_s, k_s, v_s, lse_s
):
    half = q_own.shape[0]
    for all_ref, own, rec in ((q_s, q_own, q_rec), (k_s, k_own, k_rec), (v_s, v_own, v_rec)):
        all_ref[:half, :] = own[...]
        all_ref[half:, :] = rec[...]
    masks = lane_masks(BF16)
    low, high = lane_masks(F32)
    bias = bias_ref[...]

    def block(idx, carry):
        row = pl.multiple_of(idx * SPAN, 16)
        query = q_s[pl.ds(row, SPAN), :]
        outs = []
        sums = []
        for mask in masks:
            scores = lax.dot_general(query * mask, k_s[...], NT, preferred_element_type=F32) + bias
            peak = jnp.max(scores, axis=-1, keepdims=True)
            weight = jnp.exp(scores - peak)
            total = jnp.sum(weight, axis=-1, keepdims=True)
            mixed = jnp.dot(weight.astype(BF16), v_s[...], preferred_element_type=F32)
            outs.append(mixed / total)
            sums.append(peak + jnp.log(total))
        o_ref[pl.ds(row, SPAN), :] = (outs[0] * low + outs[1] * high).astype(BF16)
        lse_s[pl.ds(row, SPAN), :] = sums[0] * low + sums[1] * high
        return carry

    lax.fori_loop(0, 2 * half // SPAN, block, 0)
    turned = jnp.transpose(lse_s[...])
    lse_ref[0, 0:8, :] = turned[0:8, :]
    lse_ref[0, 8:16, :] = turned[HEAD_DIM : HEAD_DIM + 8, :]


def backward_kernel(
    core_ref,
    q_own,
    k_own,
    v_own,
    q_rec,
    k_rec,
    v_rec,
    g_own,
    g_rec,
    o_ref,
    lse_ref,
    bias_ref,
    d_ref,
    q_s,
    k_s,
    v_s,
    g_s,
    dqt_s,
):
    half = q_own.shape[0]
    width = d_ref.shape[1] // 3
    pair = pl.program_id(0)
    cols = [pl.multiple_of(part * width + pair * 2 * HEAD_DIM, 128) for part in range(3)]
    low, high = lane_masks(BF16)
    for all_ref, own, rec in ((k_s, k_own, k_rec), (v_s, v_own, v_rec)):
        all_ref[:half, :] = own[...]
        all_ref[half:, :] = rec[...]
    for all_ref, own, rec in ((q_s, q_own, q_rec), (g_s, g_own, g_rec)):
        for head, mask in enumerate((low, high)):
            all_ref[head, :half, :] = own[...] * mask
            all_ref[head, half:, :] = rec[...] * mask
    dots_own = jnp.transpose(g_own[...].astype(F32) * o_ref[:half, :].astype(F32))
    dots_rec = jnp.transpose(g_rec[...].astype(F32) * o_ref[half:, :].astype(F32))
    dots = jnp.concatenate([dots_own, dots_rec], axis=1)
    inner = (
        jnp.sum(dots[:HEAD_DIM], axis=0, keepdims=True),
        jnp.sum(dots[HEAD_DIM:], axis=0, keepdims=True),
    )
    dqt_s[...] = jnp.zeros_like(dqt_s)

    def block(idx, carry):
        row = pl.multiple_of(idx * SPAN, 16)
        key = k_s[pl.ds(row, SPAN), :]
        value = v_s[pl.ds(row, SPAN), :]
        bias = bias_ref[pl.ds(row, SPAN), :]
        key_t = jnp.transpose(key.astype(F32)).astype(BF16)
        dk = jnp.zeros((SPAN, 2 * HEAD_DIM), F32)
        dv = jnp.zeros((SPAN, 2 * HEAD_DIM), F32)
        for head in range(2):
            query = q_s[head]
            grad = g_s[head]
            lse = lse_ref[0, 8 * head : 8 * head + 1, :]
            prob = jnp.exp(
                lax.dot_general(key, query, NT, preferred_element_type=F32) + bias - lse
            )
            g_prob = lax.dot_general(value, grad, NT, preferred_element_type=F32)
            g_score = (prob * (g_prob - inner[head])).astype(BF16)
            dv = dv + jnp.dot(prob.astype(BF16), grad, preferred_element_type=F32)
            dk = dk + jnp.dot(g_score, query, preferred_element_type=F32)
            rows = slice(HEAD_DIM * head, HEAD_DIM * (head + 1))
            dqt_s[rows, :] += jnp.dot(key_t[rows, :], g_score, preferred_element_type=F32)
        d_ref[pl.ds(row, SPAN), pl.ds(cols[1], 2 * HEAD_DIM)] = dk.astype(BF16)
        d_ref[pl.ds(row, SPAN), pl.ds(cols[2], 2 * HEAD_DIM)] = dv.astype(BF16)
        return carry

    lax.fori_loop(0, 2 * half // SPAN, block, 0)
    dq = (jnp.transpose(dqt_s[...]) * HEAD_DIM ** (-0.5)).astype(BF16)
    d_ref[:, pl.ds(cols[0], 2 * HEAD_DIM)] = dq


def call(kernel, core, args, grid, in_specs, out_specs, out_shape, scratch, flops, trans):
    moved = sum(arg.size * arg.dtype.itemsize for arg in args)
    return pl.pallas_call(
        kernel,
        grid_spec=pltpu.PrefetchScalarGridSpec(
            num_scalar_prefetch=1,
            grid=grid,
            in_specs=in_specs,
            out_specs=out_specs,
            scratch_shapes=scratch,
        ),
        out_shape=out_shape,
        cost_estimate=pl.CostEstimate(flops=flops, transcendentals=trans, bytes_accessed=moved),
        compiler_params=pltpu.CompilerParams(vmem_limit_bytes=56 * 1024 * 1024),
    )(core, *args)


def head_blocks(half, pairs, first=0):
    wide = 2 * HEAD_DIM
    own = [
        pl.BlockSpec((half, wide), lambda pair, core, at=at: (0, 2 * (at + pair + first) + core[0]))
        for at in (0, pairs, 0)
    ]
    rec = [
        pl.BlockSpec((half, wide), lambda pair, core, at=at: (0, at + pair + first))
        for at in (0, pairs, 0)
    ]
    return own + rec


def attention(core, heads, bias):
    half, width = heads[-1].shape
    wide = 2 * HEAD_DIM
    pairs = width // wide
    full = 2 * half
    ops = pairs * 2 * full * full
    return call(
        forward_kernel,
        core,
        heads + (bias.reshape(1, full),),
        (pairs,),
        head_blocks(half, pairs) + [pl.BlockSpec((1, full), lambda pair, core: (0, 0))],
        [
            pl.BlockSpec((full, wide), lambda pair, core: (0, pair)),
            pl.BlockSpec((1, 16, full), lambda pair, core: (pair, 0, 0)),
        ],
        [
            jax.ShapeDtypeStruct((full, width), BF16),
            jax.ShapeDtypeStruct((pairs, 16, full), F32),
        ],
        [pltpu.VMEM((full, wide), BF16)] * 3 + [pltpu.VMEM((full, wide), F32)],
        ops * 4 * 256,
        ops,
    )


def attention_back(core, heads, g_own, g_rec, mixed, lse, bias, first, last):
    half, width = heads[-1].shape
    wide = 2 * HEAD_DIM
    pairs = width // wide
    here = last - first
    full = 2 * half
    col = pl.BlockSpec((half, wide), lambda pair, core: (0, pair + first))
    ops = here * 2 * full * full
    return call(
        backward_kernel,
        core,
        heads + (g_own, g_rec, mixed, lse, bias.reshape(full, 1)),
        (here,),
        head_blocks(half, pairs, first)
        + [
            col,
            col,
            pl.BlockSpec((full, wide), lambda pair, core: (0, pair + first)),
            pl.BlockSpec((1, 16, full), lambda pair, core: (pair + first, 0, 0)),
            pl.BlockSpec((full, 1), lambda pair, core: (0, 0)),
        ],
        pl.BlockSpec((full, 3 * here * wide), lambda pair, core: (0, 0)),
        jax.ShapeDtypeStruct((full, 3 * here * wide), BF16),
        [
            pltpu.VMEM((2, full, wide), BF16),
            pltpu.VMEM((full, wide), BF16),
            pltpu.VMEM((full, wide), BF16),
            pltpu.VMEM((2, full, wide), BF16),
            pltpu.VMEM((wide, full), F32),
        ],
        ops * 10 * 256,
        ops,
    )


def grad_kernel(core_ref, a_own, a_rec, *refs):
    out = refs[-1]
    count = len(refs) // 2
    start = 0
    for b_own, b_rec in zip(refs[:count], refs[count:-1]):
        total = lax.dot_general(a_own[...], b_own[...], TN, preferred_element_type=F32)
        total += lax.dot_general(a_rec[...], b_rec[...], TN, preferred_element_type=F32)
        out[:, start : start + b_own.shape[1]] = total.astype(BF16)
        start += b_own.shape[1]


def weight_grad(core, args, specs, shape, tile):
    rows = 4 * SPAN
    return call(
        grad_kernel,
        core,
        args,
        (shape[0] // tile,),
        specs,
        pl.BlockSpec((tile, shape[1]), lambda i, core: (i, 0)),
        jax.ShapeDtypeStruct(shape, BF16),
        [],
        2 * rows * shape[0] * shape[1],
        0,
    )


def pick_kernel(unit, core_ref, src, dst):
    for parity in range(2):

        @pl.when(core_ref[0] == parity)
        def _():
            for idx in range(dst.shape[1] // unit):
                low = (2 * idx + 1 - parity) * unit
                dst[:, idx * unit : (idx + 1) * unit] = src[:, low : low + unit]


def pick_other(core, array, unit):
    rows, width = array.shape
    wide = 1024
    return call(
        functools.partial(pick_kernel, unit),
        core,
        (array,),
        (width // wide,),
        [pl.BlockSpec((rows, wide), lambda i, core: (0, i))],
        pl.BlockSpec((rows, wide // 2), lambda i, core: (0, i)),
        jax.ShapeDtypeStruct((rows, width // 2), array.dtype),
        [],
        0,
        0,
    )


def merge_kernel(unit, core_ref, *refs):
    dst = refs[-1]
    count = len(refs) // 2
    for parity in range(2):

        @pl.when(core_ref[0] == parity)
        def _():
            at = 0
            for own, rec in zip(refs[:count], refs[count:-1]):
                for idx in range(own.shape[1] // unit):
                    cols = slice(idx * unit, (idx + 1) * unit)
                    for side, src in enumerate((own, rec)):
                        low = at + (parity + side) % 2 * unit
                        dst[:, low : low + unit] = src[:, cols]
                    at += 2 * unit


def merge(core, owns, recs, rows, unit, steps):
    width = sum(rec.shape[1] for rec in recs)
    specs = [pl.BlockSpec((rows, rec.shape[1] // steps), lambda i, core: (0, i)) for rec in recs]
    return call(
        functools.partial(merge_kernel, unit),
        core,
        tuple(owns) + tuple(recs),
        (steps,),
        specs + specs,
        pl.BlockSpec((rows, 2 * width // steps), lambda i, core: (0, i)),
        jax.ShapeDtypeStruct((rows, 2 * width), recs[0].dtype),
        [],
        0,
        0,
    )


def gelu_parts(values):
    phi_sum = 0.5 * (1.0 + lax.erf(values * 0.7071067811865476))
    phi = jnp.exp(-0.5 * values * values) * 0.3989422804014327
    return phi_sum, phi


def norm_parts(values):
    center = values - jnp.mean(values, axis=-1, keepdims=True)
    spread = jnp.mean(center * center, axis=-1, keepdims=True)
    scale = lax.rsqrt(spread + 1e-06)
    return center * scale, scale


def norm_back(values, gain, grad):
    unit, scale = norm_parts(values)
    scaled = grad * gain
    drift = jnp.mean(scaled, axis=-1, keepdims=True)
    slope = jnp.mean(scaled * unit, axis=-1, keepdims=True)
    back = scale * (scaled - drift - unit * slope)
    return back, jnp.sum(grad * unit, axis=0), jnp.sum(grad, axis=0)


def make_step(n_shard, n_seq):
    def place(shard, seq):
        return shard * n_seq + seq

    def route(turn):
        moves = []
        for shard in range(n_shard):
            for seq in range(n_seq):
                src = place(shard, seq)
                dst = place(
                    shard // 2 * 2 + seq % 2, 2 * (shard % 2) + (turn + seq // 2) % 2
                )
                if src != dst:
                    moves.append((src, dst))
        return moves

    there = (route(0), route(1))
    back = tuple([(dst, src) for src, dst in moves] for moves in there)
    swap = [
        (place(shard, seq), place(shard ^ 1, seq))
        for shard in range(n_shard)
        for seq in range(n_seq)
    ]
    axes = ("shard", "seq")
    chips = [list(range(core, n_shard, 2)) for core in range(2)]

    def inner(
        inputs,
        teacher,
        cotangent,
        token_valid,
        image_real,
        w_qkv,
        q_bias,
        v_bias,
        w_out,
        out_bias,
        norm1_gain,
        norm1_bias,
        scale1,
        norm2_gain,
        norm2_bias,
        w_up,
        up_bias,
        w_down,
        down_bias,
        scale2,
    ):
        images, tok_dev, width = inputs.shape
        dl = q_bias.shape[0]
        ups = up_bias.shape[0] // dl
        ff = ups * width
        shard_pos = lax.axis_index("shard")
        seq_pos = lax.axis_index("seq")
        core = shard_pos % 2
        turn_out = seq_pos // 2
        turn_in = seq_pos % 2
        pad = SPAN - tok_dev
        rows = 2 * SPAN

        def move(array, turn, moves):
            stays = (core == turn_in) & (seq_pos == 2 * core + (turn + turn_out) % 2)
            return jnp.where(stays, array, lax.ppermute(array, axes, moves))

        def bring(array):
            got = [
                move(
                    lax.dynamic_index_in_dim(array, (turn + turn_out) % 2, 0, keepdims=False),
                    turn,
                    there[turn],
                )
                for turn in range(2)
            ]
            first = jnp.where(turn_in == 0, got[0], got[1])
            second = jnp.where(turn_in == 0, got[1], got[0])
            both = jnp.stack([first, second])
            return jnp.pad(both, ((0, 0), (0, pad), (0, 0))).reshape(rows, array.shape[-1])

        def give(array):
            parts = array.reshape(2, SPAN, array.shape[-1])[:, :tok_dev]
            got = [
                move(
                    lax.dynamic_index_in_dim(parts, (turn + seq_pos) % 2, 0, keepdims=False),
                    turn,
                    back[turn],
                )
                for turn in range(2)
            ]
            first = jnp.where(turn_out == 0, got[0], got[1])
            second = jnp.where(turn_out == 0, got[1], got[0])
            return jnp.stack([first, second])

        def exchange(array):
            return lax.ppermute(array, axes, swap)

        halves = dl % (2 * HEAD_DIM) == 0

        def interleave(own, other, part, axis, order=None):
            own = jnp.split(own, own.shape[axis] // part, axis)
            other = jnp.split(other, len(own), axis)
            blocks = []
            for idx in order or range(len(own)):
                mine, his = own[idx], other[idx]
                blocks.append(jnp.where(core == 0, mine, his))
                blocks.append(jnp.where(core == 0, his, mine))
            return jnp.concatenate(blocks, axis)

        def scatter(array, part, axis, order=None):
            if halves:
                return lax.psum_scatter(
                    array, "shard", scatter_dimension=0, axis_index_groups=chips, tiled=True
                )
            array = interleave(array, jnp.zeros_like(array), part, axis, order)
            return lax.psum_scatter(array, "shard", scatter_dimension=0, tiled=True)

        def z_reduce(array):
            split = (n_seq, array.shape[0] // n_seq, array.shape[1])
            got = lax.all_to_all(array.reshape(split), "seq", 0, 0, tiled=True)
            total = jnp.sum(got.astype(F32), axis=0).astype(BF16)
            got = lax.all_to_all(
                jnp.broadcast_to(total[None], split), "seq", 0, 0, tiled=True
            )
            return got.reshape(array.shape)

        def spread(array, part, order=None):
            if not halves:
                return array
            array = array.reshape(2, dl, array.shape[1])
            keep = lax.dynamic_index_in_dim(array, core, 0, keepdims=False)
            away = lax.dynamic_index_in_dim(array, 1 - core, 0, keepdims=False)
            return interleave(keep, exchange(away), part, 1, order)

        lengths = jnp.sum(token_valid, axis=1) * image_real
        sizes = jnp.stack([lengths // 64, lengths % 64], axis=1).reshape(1, 2 * images)
        sizes = jnp.pad(sizes.astype(BF16), ((0, 0), (0, dl - 2 * images)))
        small = jnp.concatenate(
            [
                jnp.stack(
                    [
                        q_bias,
                        v_bias,
                        out_bias,
                        norm1_gain,
                        norm1_bias,
                        scale1,
                        norm2_gain,
                        norm2_bias,
                        down_bias,
                        scale2,
                    ]
                ),
                up_bias.reshape(ups, dl),
                sizes,
            ],
            axis=0,
        )
        vecs = lax.all_gather(small, "shard", axis=1, tiled=True).astype(F32)
        qbias, vbias, obias, gain1, shift1, layer1, gain2, shift2, dbias, layer2 = (
            vecs[i] for i in range(10)
        )
        ubias = (
            vecs[10 : 10 + ups].reshape(ups, n_shard, dl).transpose(1, 0, 2).reshape(ff)
        )
        tails = vecs[10 + ups].reshape(n_shard, dl)[:, : 2 * images].reshape(n_shard, images, 2)
        all_len = tails[:, :, 0] * 64.0 + tails[:, :, 1]
        count = jnp.sum(all_len)
        my_len = all_len.reshape(-1)[
            (shard_pos // 2 * 2 + seq_pos // 2) * images + seq_pos % 2
        ]

        slot = jnp.arange(rows)
        offset = slot % SPAN

        def live_of(which):
            token = (which + 2 * (slot // SPAN)) * tok_dev + offset
            return (offset < tok_dev) & (token.astype(F32) < my_len)

        live = live_of(core)
        live_all = jnp.concatenate([live, live_of(1 - core)])
        key_bias = jnp.where(live_all, 0.0, DEAD).astype(F32)
        live = live[:, None]

        def gather(array):
            own = lax.all_to_all(
                jnp.broadcast_to(array[None], (n_shard // 2,) + array.shape),
                "shard",
                0,
                0,
                axis_index_groups=chips,
                tiled=True,
            )
            rec = exchange(own)
            both = [jnp.where(core == 0, own, rec), jnp.where(core == 0, rec, own)]
            return jnp.stack(both, axis=1).reshape(n_shard * array.shape[0], array.shape[1])

        qk_mat = lax.all_gather(w_qkv[:, : 2 * width], "shard", axis=0, tiled=True)
        v_mat = gather(w_qkv[:, 2 * width :])
        out_mat = gather(w_out)
        up_mat = lax.all_gather(w_up, "shard", axis=0, tiled=True)
        down_mat = lax.all_gather(w_down, "shard", axis=0, tiled=True)

        unit = 2 * HEAD_DIM
        ff_unit = max(ff // n_shard, 4 * unit)
        core_arr = core.astype(jnp.int32).reshape(1)
        x_rows = bring(inputs).astype(F32)
        normed1 = (norm_parts(x_rows)[0] * gain1 + shift1).astype(BF16)
        normed1_rec = exchange(normed1)
        qk_bias = jnp.concatenate([qbias, jnp.zeros_like(qbias)])
        scale = jnp.concatenate(
            [jnp.full((width,), HEAD_DIM ** (-0.5), BF16), jnp.ones((width,), BF16)]
        )
        qk = (jnp.dot(normed1, qk_mat, preferred_element_type=F32) + qk_bias).astype(BF16) * scale
        value = (jnp.dot(normed1, v_mat, preferred_element_type=F32) + vbias).astype(BF16)
        qk_rec = exchange(pick_other(core_arr, qk, unit))
        value_rec = exchange(pick_other(core_arr, value, unit))
        heads = (qk, qk, value, qk_rec, qk_rec, value_rec)
        mixed_mine, lse = attention(core_arr, heads, key_bias)
        both = bring(jnp.concatenate([teacher, cotangent], axis=-1))
        teach_rows = both[:, :width].astype(F32)
        cot_rows = both[:, width:].astype(F32)
        mixed = merge(core_arr, (mixed_mine,), (exchange(mixed_mine[rows:]),), rows, unit, 1)
        attn_out = jnp.dot(mixed, out_mat, preferred_element_type=F32) + obias
        resid1 = x_rows + layer1 * attn_out
        normed2 = (norm_parts(resid1)[0] * gain2 + shift2).astype(BF16)
        normed2_rec = exchange(normed2)
        pre = jnp.dot(normed2, up_mat, preferred_element_type=F32) + ubias
        act = (pre * gelu_parts(pre)[0]).astype(BF16)
        act_rec = exchange(act)
        branch = jnp.dot(act, down_mat, preferred_element_type=F32) + dbias
        resid2 = resid1 + layer2 * branch
        out_rows = jnp.where(live, resid2, x_rows)
        diff = jnp.where(live, out_rows - teach_rows, 0.0)
        err = jnp.sum(diff * diff)
        result = give(out_rows.astype(BF16))

        g_out = cot_rows + 2.0 * diff / (count * width)
        g_keep = jnp.where(live, g_out, 0.0)
        g_pass = g_out - g_keep
        d_scale2 = jnp.sum(g_keep * branch, axis=0)
        g_branch = (g_keep * layer2).astype(BF16)
        d_down_bias = jnp.sum(g_branch.astype(F32), axis=0)
        g_branch_rec = exchange(g_branch)

        tile = 2 * unit
        whole = pl.BlockSpec((rows, width), lambda i, core: (0, 0))
        strip = pl.BlockSpec((rows, tile), lambda i, core: (0, i))
        per = ff_unit // tile
        act_spec = pl.BlockSpec(
            (rows, tile), lambda i, core: (0, (2 * (i // per) + core[0]) * per + i % per)
        )
        w_down_part = weight_grad(
            core_arr,
            (act, act_rec, g_branch, g_branch_rec),
            [act_spec, act_spec, whole, whole],
            (ff // 2, width),
            tile,
        )
        p_down = scatter(w_down_part, ff_unit, 0)
        g_hidden = jnp.einsum("rd,fd->rf", g_branch, down_mat, preferred_element_type=F32)
        phi_sum, phi = gelu_parts(pre)
        g_pre = (g_hidden * (phi_sum + pre * phi)).astype(BF16)
        d_up_bias = jnp.sum(g_pre.astype(F32), axis=0)
        g_pre_rec = exchange(g_pre)
        n_units = ff // ff_unit // 2
        w_up_part = weight_grad(
            core_arr,
            (normed2, normed2_rec) + (g_pre,) * n_units + (g_pre_rec,) * n_units,
            [strip, strip]
            + [
                pl.BlockSpec((rows, ff_unit), lambda i, core, j=j: (0, 2 * j + core[0]))
                for j in range(n_units)
            ]
            * 2,
            (width, ff // 2),
            tile,
        )
        p_up = scatter(w_up_part, ff_unit, 1)
        g_norm2 = jnp.einsum("rf,df->rd", g_pre, up_mat, preferred_element_type=F32)
        g_ln2, d_gain2, d_shift2 = norm_back(resid1, gain2, g_norm2)
        g_resid1 = g_keep + g_ln2
        d_scale1 = jnp.sum(g_resid1 * attn_out, axis=0)
        g_attn = (g_resid1 * layer1).astype(BF16)
        d_out_bias = jnp.sum(g_attn.astype(F32), axis=0)
        g_attn_rec = exchange(g_attn)
        out_mine = lax.dynamic_index_in_dim(
            out_mat.reshape(width // unit // 2, 2, unit, width), core, 1, keepdims=False
        ).reshape(width // 2, width)

        def mixed_grad(array):
            return jnp.einsum("rd,cd->rc", array, out_mine, preferred_element_type=F32).astype(BF16)

        w_out_part = weight_grad(
            core_arr,
            (mixed_mine, mixed_mine, g_attn, g_attn_rec),
            [strip, pl.BlockSpec((rows, tile), lambda i, core: (1, i)), whole, whole],
            (width // 2, width),
            tile,
        )
        p_out = scatter(w_out_part, unit, 0)
        g_mine = (mixed_grad(g_attn), mixed_grad(g_attn_rec))
        pairs = width // 2 // unit
        g_alls = [
            attention_back(core_arr, heads, *g_mine, mixed_mine, lse, key_bias, first, last)
            for first, last in ((0, 1), (1, pairs - 1), (pairs - 1, pairs))
        ]
        g_recs = [exchange(part[rows:]) for part in g_alls]
        order = []
        for part in range(3):
            for first, last in ((0, 1), (1, pairs - 1), (pairs - 1, pairs)):
                order += [3 * first + part * (last - first) + idx for idx in range(last - first)]
        w_qkv_part = weight_grad(
            core_arr,
            (normed1, normed1_rec) + tuple(g_alls) * 2,
            [strip, strip]
            + [
                pl.BlockSpec((rows, part.shape[1]), lambda i, core, side=side: (side, 0))
                for side in range(2)
                for part in g_alls
            ],
            (width, 3 * width // 2),
            tile,
        )
        p_qkv = scatter(w_qkv_part, unit, 1, order)
        g_qkv = merge(core_arr, g_alls, g_recs, rows, unit, 3)
        d_qkv_bias = jnp.sum(g_qkv.astype(F32), axis=0)
        g_norm1 = jnp.einsum(
            "re,de->rd", g_qkv[:, : 2 * width], qk_mat, preferred_element_type=F32
        ) + jnp.einsum("re,de->rd", g_qkv[:, 2 * width :], v_mat, preferred_element_type=F32)
        g_ln1, d_gain1, d_shift1 = norm_back(x_rows, gain1, g_norm1)
        g_in = give((g_pass + g_resid1 + g_ln1).astype(BF16)).astype(F32)

        p_down = z_reduce(p_down)
        p_up = z_reduce(p_up)
        p_out, p_qkv = lax.psum((p_out, p_qkv), "seq")
        p_up = spread(p_up, ff_unit)
        p_qkv = spread(p_qkv, unit, order)
        sums = jnp.concatenate(
            [
                jnp.stack(
                    [
                        d_qkv_bias[:width],
                        d_qkv_bias[2 * width :],
                        d_out_bias,
                        d_gain1,
                        d_shift1,
                        d_scale1,
                        d_gain2,
                        d_shift2,
                        d_down_bias,
                        d_scale2,
                    ]
                ),
                d_up_bias.reshape(n_shard, ups, dl).transpose(1, 0, 2).reshape(ups, width),
                jnp.full((1, width), err),
            ],
            axis=0,
        )
        kinds = sums.shape[0]
        sums = sums.reshape(kinds, n_shard, 1, dl).transpose(1, 2, 0, 3)
        sums = jnp.broadcast_to(sums, (n_shard, n_seq, kinds, dl))
        sums = lax.all_to_all(
            sums.reshape(n_shard * n_seq, kinds, dl), axes, 0, 0, tiled=True
        )
        mine = jnp.sum(sums, axis=0)
        loss = mine[10 + ups, 0] / (count * width)
        (
            s_qb, s_vb, s_ob, s_g1, s_b1, s_l1, s_g2, s_b2, s_db, s_l2
        ) = (mine[i] for i in range(10))
        s_ub = mine[10 : 10 + ups].reshape(ups * dl)
        return (
            result,
            loss,
            g_in,
            p_qkv.astype(F32),
            s_qb,
            s_vb,
            p_out.astype(F32),
            s_ob,
            s_g1,
            s_b1,
            s_l1,
            s_g2,
            s_b2,
            p_up.astype(F32),
            s_ub,
            p_down.astype(F32),
            s_db,
            s_l2,
        )

    return inner


def solution(mesh):
    tokens = P("shard", "seq", None)
    matrix = P("shard", None)
    vector = P("shard")
    in_specs = (
        tokens,
        tokens,
        tokens,
        matrix,
        vector,
        matrix,
        vector,
        vector,
        matrix,
        vector,
        vector,
        vector,
        vector,
        vector,
        vector,
        matrix,
        vector,
        matrix,
        vector,
        vector,
    )
    out_specs = (
        tokens,
        P(),
        tokens,
        matrix,
        vector,
        vector,
        matrix,
        vector,
        vector,
        vector,
        vector,
        vector,
        vector,
        matrix,
        vector,
        matrix,
        vector,
        vector,
    )
    return jax.shard_map(
        make_step(mesh.shape["shard"], mesh.shape["seq"]),
        mesh=mesh,
        in_specs=in_specs,
        out_specs=out_specs,
        check_vma=False,
    )
```

```python
import functools

import jax
import jax.numpy as jnp
from jax import lax
from jax.experimental import pallas as pl
from jax.experimental.pallas import tpu as pltpu
from jax.sharding import PartitionSpec as P

HEAD_DIM = 64
DEAD = -1000000000.0
SPAN = 352
F32 = jnp.float32
BF16 = jnp.bfloat16
NT = (((1,), (1,)), ((), ()))
TN = (((0,), (0,)), ((), ()))


def lane_masks(dtype):
    lane = lax.broadcasted_iota(jnp.int32, (1, 2 * HEAD_DIM), 1)
    low = jnp.where(lane < HEAD_DIM, 1.0, 0.0).astype(F32)
    return low.astype(dtype), (1.0 - low).astype(dtype)


def store_rows(own, away, idx, cols, value):
    count = own.shape[0] // SPAN
    row = pl.multiple_of(lax.rem(idx, count) * SPAN, 16)

    @pl.when(idx < count)
    def _():
        own[pl.ds(row, SPAN), cols] = value

    @pl.when(idx >= count)
    def _():
        away[pl.ds(row, SPAN), cols] = value


def forward_kernel(
    core_ref, q_own, k_own, v_own, q_rec, k_rec, v_rec, bias_ref, o_own, o_away, lse_ref, q_s, k_s, v_s, lse_s
):
    half = q_own.shape[0]
    for all_ref, own, rec in ((q_s, q_own, q_rec), (k_s, k_own, k_rec), (v_s, v_own, v_rec)):
        all_ref[:half, :] = own[...]
        all_ref[half:, :] = rec[...]
    masks = lane_masks(BF16)
    low, high = lane_masks(F32)
    bias = bias_ref[...]

    def block(idx, carry):
        row = pl.multiple_of(idx * SPAN, 16)
        query = q_s[pl.ds(row, SPAN), :]
        outs = []
        sums = []
        for mask in masks:
            scores = lax.dot_general(query * mask, k_s[...], NT, preferred_element_type=F32) + bias
            peak = jnp.max(scores, axis=-1, keepdims=True)
            weight = jnp.exp(scores - peak)
            total = jnp.sum(weight, axis=-1, keepdims=True)
            mixed = jnp.dot(weight.astype(BF16), v_s[...], preferred_element_type=F32)
            outs.append(mixed / total)
            sums.append(peak + jnp.log(total))
        store_rows(o_own, o_away, idx, slice(None), (outs[0] * low + outs[1] * high).astype(BF16))
        lse_s[pl.ds(row, SPAN), :] = sums[0] * low + sums[1] * high
        return carry

    lax.fori_loop(0, 2 * half // SPAN, block, 0)
    turned = jnp.transpose(lse_s[...])
    lse_ref[0, 0:8, :] = turned[0:8, :]
    lse_ref[0, 8:16, :] = turned[HEAD_DIM : HEAD_DIM + 8, :]


def backward_kernel(
    core_ref,
    q_own,
    k_own,
    v_own,
    q_rec,
    k_rec,
    v_rec,
    g_own,
    g_rec,
    o_own,
    o_away,
    lse_ref,
    bias_ref,
    d_own,
    d_away,
    q_s,
    k_s,
    v_s,
    g_s,
    dqt_s,
):
    half = q_own.shape[0]
    width = d_own.shape[1] // 3
    pair = pl.program_id(0)
    cols = [pl.multiple_of(part * width + pair * 2 * HEAD_DIM, 128) for part in range(3)]
    low, high = lane_masks(BF16)
    for all_ref, own, rec in ((k_s, k_own, k_rec), (v_s, v_own, v_rec)):
        all_ref[:half, :] = own[...]
        all_ref[half:, :] = rec[...]
    for all_ref, own, rec in ((q_s, q_own, q_rec), (g_s, g_own, g_rec)):
        for head, mask in enumerate((low, high)):
            all_ref[head, :half, :] = own[...] * mask
            all_ref[head, half:, :] = rec[...] * mask
    dots_own = jnp.transpose(g_own[...].astype(F32) * o_own[...].astype(F32))
    dots_rec = jnp.transpose(g_rec[...].astype(F32) * o_away[...].astype(F32))
    dots = jnp.concatenate([dots_own, dots_rec], axis=1)
    inner = (
        jnp.sum(dots[:HEAD_DIM], axis=0, keepdims=True),
        jnp.sum(dots[HEAD_DIM:], axis=0, keepdims=True),
    )
    dqt_s[...] = jnp.zeros_like(dqt_s)

    def block(idx, carry):
        row = pl.multiple_of(idx * SPAN, 16)
        key = k_s[pl.ds(row, SPAN), :]
        value = v_s[pl.ds(row, SPAN), :]
        bias = bias_ref[pl.ds(row, SPAN), :]
        key_t = jnp.transpose(key.astype(F32)).astype(BF16)
        dk = jnp.zeros((SPAN, 2 * HEAD_DIM), F32)
        dv = jnp.zeros((SPAN, 2 * HEAD_DIM), F32)
        for head in range(2):
            query = q_s[head]
            grad = g_s[head]
            lse = lse_ref[0, 8 * head : 8 * head + 1, :]
            prob = jnp.exp(
                lax.dot_general(key, query, NT, preferred_element_type=F32) + bias - lse
            )
            g_prob = lax.dot_general(value, grad, NT, preferred_element_type=F32)
            g_score = (prob * (g_prob - inner[head])).astype(BF16)
            dv = dv + jnp.dot(prob.astype(BF16), grad, preferred_element_type=F32)
            dk = dk + jnp.dot(g_score, query, preferred_element_type=F32)
            rows = slice(HEAD_DIM * head, HEAD_DIM * (head + 1))
            dqt_s[rows, :] += jnp.dot(key_t[rows, :], g_score, preferred_element_type=F32)
        store_rows(d_own, d_away, idx, pl.ds(cols[1], 2 * HEAD_DIM), dk.astype(BF16))
        store_rows(d_own, d_away, idx, pl.ds(cols[2], 2 * HEAD_DIM), dv.astype(BF16))
        return carry

    lax.fori_loop(0, 2 * half // SPAN, block, 0)
    dq = (jnp.transpose(dqt_s[...]) * HEAD_DIM ** (-0.5)).astype(BF16)
    d_own[:, pl.ds(cols[0], 2 * HEAD_DIM)] = dq[:half, :]
    d_away[:, pl.ds(cols[0], 2 * HEAD_DIM)] = dq[half:, :]


def call(kernel, core, args, grid, in_specs, out_specs, out_shape, scratch, flops, trans):
    moved = sum(arg.size * arg.dtype.itemsize for arg in args)
    return pl.pallas_call(
        kernel,
        grid_spec=pltpu.PrefetchScalarGridSpec(
            num_scalar_prefetch=1,
            grid=grid,
            in_specs=in_specs,
            out_specs=out_specs,
            scratch_shapes=scratch,
        ),
        out_shape=out_shape,
        cost_estimate=pl.CostEstimate(flops=flops, transcendentals=trans, bytes_accessed=moved),
        compiler_params=pltpu.CompilerParams(vmem_limit_bytes=56 * 1024 * 1024),
    )(core, *args)


def head_blocks(half, pairs, first=0):
    wide = 2 * HEAD_DIM
    own = [
        pl.BlockSpec((half, wide), lambda pair, core, at=at: (0, 2 * (at + pair + first) + core[0]))
        for at in (0, pairs, 2 * pairs)
    ]
    rec = [
        pl.BlockSpec((half, wide), lambda pair, core, at=at: (0, at + pair + first))
        for at in (0, pairs, 2 * pairs)
    ]
    return own + rec


def attention(core, heads, bias):
    half, width = heads[-1].shape[0], heads[-1].shape[1] // 3
    wide = 2 * HEAD_DIM
    pairs = width // wide
    full = 2 * half
    ops = pairs * 2 * full * full
    return call(
        forward_kernel,
        core,
        heads + (bias.reshape(1, full),),
        (pairs,),
        head_blocks(half, pairs) + [pl.BlockSpec((1, full), lambda pair, core: (0, 0))],
        [
            pl.BlockSpec((half, wide), lambda pair, core: (0, pair)),
            pl.BlockSpec((half, wide), lambda pair, core: (0, pair)),
            pl.BlockSpec((1, 16, full), lambda pair, core: (pair, 0, 0)),
        ],
        [
            jax.ShapeDtypeStruct((half, width), BF16),
            jax.ShapeDtypeStruct((half, width), BF16),
            jax.ShapeDtypeStruct((pairs, 16, full), F32),
        ],
        [pltpu.VMEM((full, wide), BF16)] * 3 + [pltpu.VMEM((full, wide), F32)],
        ops * 4 * 256,
        ops,
    )


def attention_back(core, heads, g_own, g_rec, o_own, o_away, lse, bias, first, last):
    half, width = heads[-1].shape[0], heads[-1].shape[1] // 3
    wide = 2 * HEAD_DIM
    pairs = width // wide
    here = last - first
    full = 2 * half
    col = pl.BlockSpec((half, wide), lambda pair, core: (0, pair + first))
    ops = here * 2 * full * full
    return call(
        backward_kernel,
        core,
        heads + (g_own, g_rec, o_own, o_away, lse, bias.reshape(full, 1)),
        (here,),
        head_blocks(half, pairs, first)
        + [
            col,
            col,
            col,
            col,
            pl.BlockSpec((1, 16, full), lambda pair, core: (pair + first, 0, 0)),
            pl.BlockSpec((full, 1), lambda pair, core: (0, 0)),
        ],
        [pl.BlockSpec((half, 3 * here * wide), lambda pair, core: (0, 0))] * 2,
        [jax.ShapeDtypeStruct((half, 3 * here * wide), BF16)] * 2,
        [
            pltpu.VMEM((2, full, wide), BF16),
            pltpu.VMEM((full, wide), BF16),
            pltpu.VMEM((full, wide), BF16),
            pltpu.VMEM((2, full, wide), BF16),
            pltpu.VMEM((wide, full), F32),
        ],
        ops * 10 * 256,
        ops,
    )


def grad_kernel(core_ref, a_own, a_rec, *refs):
    out = refs[-1]
    count = len(refs) // 2
    start = 0
    for b_own, b_rec in zip(refs[:count], refs[count:-1]):
        total = lax.dot_general(a_own[...], b_own[...], TN, preferred_element_type=F32)
        total += lax.dot_general(a_rec[...], b_rec[...], TN, preferred_element_type=F32)
        out[:, start : start + b_own.shape[1]] = total.astype(BF16)
        start += b_own.shape[1]


def weight_grad(core, args, specs, shape, tile):
    rows = 4 * SPAN
    return call(
        grad_kernel,
        core,
        args,
        (shape[0] // tile,),
        specs,
        pl.BlockSpec((tile, shape[1]), lambda i, core: (i, 0)),
        jax.ShapeDtypeStruct(shape, BF16),
        [],
        2 * rows * shape[0] * shape[1],
        0,
    )


def pick_kernel(unit, core_ref, src, dst):
    for parity in range(2):

        @pl.when(core_ref[0] == parity)
        def _():
            for idx in range(dst.shape[1] // unit):
                low = (2 * idx + 1 - parity) * unit
                dst[:, idx * unit : (idx + 1) * unit] = src[:, low : low + unit]


def pick_other(core, array, unit):
    rows, width = array.shape
    wide = 1024
    return call(
        functools.partial(pick_kernel, unit),
        core,
        (array,),
        (width // wide,),
        [pl.BlockSpec((rows, wide), lambda i, core: (0, i))],
        pl.BlockSpec((rows, wide // 2), lambda i, core: (0, i)),
        jax.ShapeDtypeStruct((rows, width // 2), array.dtype),
        [],
        0,
        0,
    )


def merge_kernel(unit, core_ref, *refs):
    dst = refs[-1]
    count = len(refs) // 2
    for parity in range(2):

        @pl.when(core_ref[0] == parity)
        def _():
            at = 0
            for own, rec in zip(refs[:count], refs[count:-1]):
                for idx in range(own.shape[1] // unit):
                    cols = slice(idx * unit, (idx + 1) * unit)
                    for side, src in enumerate((own, rec)):
                        low = at + (parity + side) % 2 * unit
                        dst[:, low : low + unit] = src[:, cols]
                    at += 2 * unit


def merge(core, owns, recs, rows, unit, steps):
    width = sum(rec.shape[1] for rec in recs)
    specs = [pl.BlockSpec((rows, rec.shape[1] // steps), lambda i, core: (0, i)) for rec in recs]
    return call(
        functools.partial(merge_kernel, unit),
        core,
        tuple(owns) + tuple(recs),
        (steps,),
        specs + specs,
        pl.BlockSpec((rows, 2 * width // steps), lambda i, core: (0, i)),
        jax.ShapeDtypeStruct((rows, 2 * width), recs[0].dtype),
        [],
        0,
        0,
    )


def gelu_parts(values):
    phi_sum = 0.5 * (1.0 + lax.erf(values * 0.7071067811865476))
    phi = jnp.exp(-0.5 * values * values) * 0.3989422804014327
    return phi_sum, phi


def norm_parts(values):
    center = values - jnp.mean(values, axis=-1, keepdims=True)
    spread = jnp.mean(center * center, axis=-1, keepdims=True)
    scale = lax.rsqrt(spread + 1e-06)
    return center * scale, scale


def norm_back(values, gain, grad):
    unit, scale = norm_parts(values)
    scaled = grad * gain
    drift = jnp.mean(scaled, axis=-1, keepdims=True)
    slope = jnp.mean(scaled * unit, axis=-1, keepdims=True)
    back = scale * (scaled - drift - unit * slope)
    return back, jnp.sum(grad * unit, axis=0), jnp.sum(grad, axis=0)


def make_step(n_shard, n_seq):
    def place(shard, seq):
        return shard * n_seq + seq

    def route(turn):
        moves = []
        for shard in range(n_shard):
            for seq in range(n_seq):
                src = place(shard, seq)
                dst = place(
                    shard // 2 * 2 + seq % 2, 2 * (shard % 2) + (turn + seq // 2) % 2
                )
                if src != dst:
                    moves.append((src, dst))
        return moves

    there = (route(0), route(1))
    back = tuple([(dst, src) for src, dst in moves] for moves in there)
    swap = [
        (place(shard, seq), place(shard ^ 1, seq))
        for shard in range(n_shard)
        for seq in range(n_seq)
    ]
    axes = ("shard", "seq")
    chips = [list(range(core, n_shard, 2)) for core in range(2)]

    def inner(
        inputs,
        teacher,
        cotangent,
        token_valid,
        image_real,
        w_qkv,
        q_bias,
        v_bias,
        w_out,
        out_bias,
        norm1_gain,
        norm1_bias,
        scale1,
        norm2_gain,
        norm2_bias,
        w_up,
        up_bias,
        w_down,
        down_bias,
        scale2,
    ):
        images, tok_dev, width = inputs.shape
        dl = q_bias.shape[0]
        ups = up_bias.shape[0] // dl
        ff = ups * width
        shard_pos = lax.axis_index("shard")
        seq_pos = lax.axis_index("seq")
        core = shard_pos % 2
        turn_out = seq_pos // 2
        turn_in = seq_pos % 2
        pad = SPAN - tok_dev
        rows = 2 * SPAN

        def move(array, turn, moves):
            stays = (core == turn_in) & (seq_pos == 2 * core + (turn + turn_out) % 2)
            return jnp.where(stays, array, lax.ppermute(array, axes, moves))

        def bring(array):
            got = [
                move(
                    lax.dynamic_index_in_dim(array, (turn + turn_out) % 2, 0, keepdims=False),
                    turn,
                    there[turn],
                )
                for turn in range(2)
            ]
            first = jnp.where(turn_in == 0, got[0], got[1])
            second = jnp.where(turn_in == 0, got[1], got[0])
            both = jnp.stack([first, second])
            return jnp.pad(both, ((0, 0), (0, pad), (0, 0))).reshape(rows, array.shape[-1])

        def give(array):
            parts = array.reshape(2, SPAN, array.shape[-1])[:, :tok_dev]
            got = [
                move(
                    lax.dynamic_index_in_dim(parts, (turn + seq_pos) % 2, 0, keepdims=False),
                    turn,
                    back[turn],
                )
                for turn in range(2)
            ]
            first = jnp.where(turn_out == 0, got[0], got[1])
            second = jnp.where(turn_out == 0, got[1], got[0])
            return jnp.stack([first, second])

        def exchange(array):
            return lax.ppermute(array, axes, swap)

        halves = dl % (2 * HEAD_DIM) == 0

        def interleave(own, other, part, axis, order=None):
            own = jnp.split(own, own.shape[axis] // part, axis)
            other = jnp.split(other, len(own), axis)
            blocks = []
            for idx in order or range(len(own)):
                mine, his = own[idx], other[idx]
                blocks.append(jnp.where(core == 0, mine, his))
                blocks.append(jnp.where(core == 0, his, mine))
            return jnp.concatenate(blocks, axis)

        def scatter(array, part, axis, order=None):
            if halves:
                return lax.psum_scatter(
                    array, "shard", scatter_dimension=0, axis_index_groups=chips, tiled=True
                )
            array = interleave(array, jnp.zeros_like(array), part, axis, order)
            return lax.psum_scatter(array, "shard", scatter_dimension=0, tiled=True)

        def z_reduce(array):
            split = (n_seq, array.shape[0] // n_seq, array.shape[1])
            got = lax.all_to_all(array.reshape(split), "seq", 0, 0, tiled=True)
            total = jnp.sum(got.astype(F32), axis=0).astype(BF16)
            got = lax.all_to_all(
                jnp.broadcast_to(total[None], split), "seq", 0, 0, tiled=True
            )
            return got.reshape(array.shape)

        def spread(array, part, order=None):
            if not halves:
                return array
            array = array.reshape(2, dl, array.shape[1])
            keep = lax.dynamic_index_in_dim(array, core, 0, keepdims=False)
            away = lax.dynamic_index_in_dim(array, 1 - core, 0, keepdims=False)
            return interleave(keep, exchange(away), part, 1, order)

        lengths = jnp.sum(token_valid, axis=1) * image_real
        sizes = jnp.stack([lengths // 64, lengths % 64], axis=1).reshape(1, 2 * images)
        sizes = jnp.pad(sizes.astype(BF16), ((0, 0), (0, dl - 2 * images)))
        small = jnp.concatenate(
            [
                jnp.stack(
                    [
                        q_bias,
                        v_bias,
                        out_bias,
                        norm1_gain,
                        norm1_bias,
                        scale1,
                        norm2_gain,
                        norm2_bias,
                        down_bias,
                        scale2,
                    ]
                ),
                up_bias.reshape(ups, dl),
                sizes,
            ],
            axis=0,
        )
        vecs = lax.all_gather(small, "shard", axis=1, tiled=True).astype(F32)
        qbias, vbias, obias, gain1, shift1, layer1, gain2, shift2, dbias, layer2 = (
            vecs[i] for i in range(10)
        )
        ubias = (
            vecs[10 : 10 + ups].reshape(ups, n_shard, dl).transpose(1, 0, 2).reshape(ff)
        )
        tails = vecs[10 + ups].reshape(n_shard, dl)[:, : 2 * images].reshape(n_shard, images, 2)
        all_len = tails[:, :, 0] * 64.0 + tails[:, :, 1]
        count = jnp.sum(all_len)
        my_len = all_len.reshape(-1)[
            (shard_pos // 2 * 2 + seq_pos // 2) * images + seq_pos % 2
        ]

        slot = jnp.arange(rows)
        offset = slot % SPAN

        def live_of(which):
            token = (which + 2 * (slot // SPAN)) * tok_dev + offset
            return (offset < tok_dev) & (token.astype(F32) < my_len)

        live = live_of(core)
        live_all = jnp.concatenate([live, live_of(1 - core)])
        key_bias = jnp.where(live_all, 0.0, DEAD).astype(F32)
        live = live[:, None]

        def gather(array):
            own = lax.all_to_all(
                jnp.broadcast_to(array[None], (n_shard // 2,) + array.shape),
                "shard",
                0,
                0,
                axis_index_groups=chips,
                tiled=True,
            )
            rec = exchange(own)
            both = [jnp.where(core == 0, own, rec), jnp.where(core == 0, rec, own)]
            return jnp.stack(both, axis=1).reshape(n_shard * array.shape[0], array.shape[1])

        qkv_mat = lax.all_gather(w_qkv, "shard", axis=0, tiled=True)
        out_mat = gather(w_out)
        up_mat = lax.all_gather(w_up, "shard", axis=0, tiled=True)
        down_mat = lax.all_gather(w_down, "shard", axis=0, tiled=True)

        unit = 2 * HEAD_DIM
        ff_unit = max(ff // n_shard, 4 * unit)
        core_arr = core.astype(jnp.int32).reshape(1)
        x_rows = bring(inputs).astype(F32)
        normed1 = (norm_parts(x_rows)[0] * gain1 + shift1).astype(BF16)
        normed1_rec = exchange(normed1)
        qkv_bias = jnp.concatenate([qbias, jnp.zeros_like(qbias), vbias])
        scale = jnp.concatenate(
            [jnp.full((width,), HEAD_DIM ** (-0.5), BF16), jnp.ones((2 * width,), BF16)]
        )
        qkv = (jnp.dot(normed1, qkv_mat, preferred_element_type=F32) + qkv_bias).astype(BF16) * scale
        rec = exchange(pick_other(core_arr, qkv, unit))
        heads = (qkv, qkv, qkv, rec, rec, rec)
        mixed_own, mixed_away, lse = attention(core_arr, heads, key_bias)
        both = bring(jnp.concatenate([teacher, cotangent], axis=-1))
        teach_rows = both[:, :width].astype(F32)
        cot_rows = both[:, width:].astype(F32)
        mixed = merge(core_arr, (mixed_own,), (exchange(mixed_away),), rows, unit, 1)
        attn_out = jnp.dot(mixed, out_mat, preferred_element_type=F32) + obias
        resid1 = x_rows + layer1 * attn_out
        normed2 = (norm_parts(resid1)[0] * gain2 + shift2).astype(BF16)
        normed2_rec = exchange(normed2)
        pre = jnp.dot(normed2, up_mat, preferred_element_type=F32) + ubias
        act = (pre * gelu_parts(pre)[0]).astype(BF16)
        act_rec = exchange(act)
        branch = jnp.dot(act, down_mat, preferred_element_type=F32) + dbias
        resid2 = resid1 + layer2 * branch
        out_rows = jnp.where(live, resid2, x_rows)
        diff = jnp.where(live, out_rows - teach_rows, 0.0)
        err = jnp.sum(diff * diff)
        result = give(out_rows.astype(BF16))

        g_out = cot_rows + 2.0 * diff / (count * width)
        g_keep = jnp.where(live, g_out, 0.0)
        g_pass = g_out - g_keep
        d_scale2 = jnp.sum(g_keep * branch, axis=0)
        g_branch = (g_keep * layer2).astype(BF16)
        d_down_bias = jnp.sum(g_branch.astype(F32), axis=0)
        g_branch_rec = exchange(g_branch)

        tile = 2 * unit
        whole = pl.BlockSpec((rows, width), lambda i, core: (0, 0))
        strip = pl.BlockSpec((rows, tile), lambda i, core: (0, i))
        per = ff_unit // tile
        act_spec = pl.BlockSpec(
            (rows, tile), lambda i, core: (0, (2 * (i // per) + core[0]) * per + i % per)
        )
        w_down_part = weight_grad(
            core_arr,
            (act, act_rec, g_branch, g_branch_rec),
            [act_spec, act_spec, whole, whole],
            (ff // 2, width),
            tile,
        )
        p_down = scatter(w_down_part, ff_unit, 0)
        g_hidden = jnp.einsum("rd,fd->rf", g_branch, down_mat, preferred_element_type=F32)
        phi_sum, phi = gelu_parts(pre)
        g_pre = (g_hidden * (phi_sum + pre * phi)).astype(BF16)
        d_up_bias = jnp.sum(g_pre.astype(F32), axis=0)
        g_pre_rec = exchange(g_pre)
        n_units = ff // ff_unit // 2
        w_up_part = weight_grad(
            core_arr,
            (normed2, normed2_rec) + (g_pre,) * n_units + (g_pre_rec,) * n_units,
            [strip, strip]
            + [
                pl.BlockSpec((rows, ff_unit), lambda i, core, j=j: (0, 2 * j + core[0]))
                for j in range(n_units)
            ]
            * 2,
            (width, ff // 2),
            tile,
        )
        p_up = scatter(w_up_part, ff_unit, 1)
        g_norm2 = jnp.einsum("rf,df->rd", g_pre, up_mat, preferred_element_type=F32)
        g_ln2, d_gain2, d_shift2 = norm_back(resid1, gain2, g_norm2)
        g_resid1 = g_keep + g_ln2
        d_scale1 = jnp.sum(g_resid1 * attn_out, axis=0)
        g_attn = (g_resid1 * layer1).astype(BF16)
        d_out_bias = jnp.sum(g_attn.astype(F32), axis=0)
        g_attn_rec = exchange(g_attn)
        out_mine = lax.dynamic_index_in_dim(
            out_mat.reshape(width // unit // 2, 2, unit, width), core, 1, keepdims=False
        ).reshape(width // 2, width)

        def mixed_grad(array):
            return jnp.einsum("rd,cd->rc", array, out_mine, preferred_element_type=F32).astype(BF16)

        w_out_part = weight_grad(
            core_arr,
            (mixed_own, mixed_away, g_attn, g_attn_rec),
            [strip, strip, whole, whole],
            (width // 2, width),
            tile,
        )
        p_out = scatter(w_out_part, unit, 0)
        g_mine = (mixed_grad(g_attn), mixed_grad(g_attn_rec))
        pairs = width // 2 // unit
        g_alls = [
            attention_back(
                core_arr, heads, *g_mine, mixed_own, mixed_away, lse, key_bias, first, last
            )
            for first, last in ((0, 1), (1, pairs - 1), (pairs - 1, pairs))
        ]
        g_owns = [part[0] for part in g_alls]
        g_aways = [part[1] for part in g_alls]
        g_recs = [exchange(part) for part in g_aways]
        order = []
        for part in range(3):
            for first, last in ((0, 1), (1, pairs - 1), (pairs - 1, pairs)):
                order += [3 * first + part * (last - first) + idx for idx in range(last - first)]
        w_qkv_part = weight_grad(
            core_arr,
            (normed1, normed1_rec) + tuple(g_owns) + tuple(g_aways),
            [strip, strip]
            + [pl.BlockSpec((rows, part.shape[1]), lambda i, core: (0, 0)) for part in g_owns] * 2,
            (width, 3 * width // 2),
            tile,
        )
        p_qkv = scatter(w_qkv_part, unit, 1, order)
        g_qkv = merge(core_arr, g_owns, g_recs, rows, unit, 3)
        d_qkv_bias = jnp.sum(g_qkv.astype(F32), axis=0)
        g_norm1 = jnp.einsum("re,de->rd", g_qkv, qkv_mat, preferred_element_type=F32)
        g_ln1, d_gain1, d_shift1 = norm_back(x_rows, gain1, g_norm1)
        g_in = (g_pass + g_resid1 + g_ln1).astype(BF16)
        g_in = give(g_in).astype(F32)

        p_down = z_reduce(p_down)
        p_up = z_reduce(p_up)
        p_out, p_qkv = lax.psum((p_out, p_qkv), "seq")
        p_up = spread(p_up, ff_unit)
        p_qkv = spread(p_qkv, unit, order)
        sums = jnp.concatenate(
            [
                jnp.stack(
                    [
                        d_qkv_bias[:width],
                        d_qkv_bias[2 * width :],
                        d_out_bias,
                        d_gain1,
                        d_shift1,
                        d_scale1,
                        d_gain2,
                        d_shift2,
                        d_down_bias,
                        d_scale2,
                    ]
                ),
                d_up_bias.reshape(n_shard, ups, dl).transpose(1, 0, 2).reshape(ups, width),
                jnp.full((1, width), err),
            ],
            axis=0,
        )
        kinds = sums.shape[0]
        sums = sums.reshape(kinds, n_shard, 1, dl).transpose(1, 2, 0, 3)
        sums = jnp.broadcast_to(sums, (n_shard, n_seq, kinds, dl))
        sums = lax.all_to_all(
            sums.reshape(n_shard * n_seq, kinds, dl), axes, 0, 0, tiled=True
        )
        mine = jnp.sum(sums, axis=0)
        loss = mine[10 + ups, 0] / (count * width)
        (
            s_qb, s_vb, s_ob, s_g1, s_b1, s_l1, s_g2, s_b2, s_db, s_l2
        ) = (mine[i] for i in range(10))
        s_ub = mine[10 : 10 + ups].reshape(ups * dl)
        return (
            result,
            loss,
            g_in,
            p_qkv.astype(F32),
            s_qb,
            s_vb,
            p_out.astype(F32),
            s_ob,
            s_g1,
            s_b1,
            s_l1,
            s_g2,
            s_b2,
            p_up.astype(F32),
            s_ub,
            p_down.astype(F32),
            s_db,
            s_l2,
        )

    return inner


def solution(mesh):
    tokens = P("shard", "seq", None)
    matrix = P("shard", None)
    vector = P("shard")
    in_specs = (
        tokens,
        tokens,
        tokens,
        matrix,
        vector,
        matrix,
        vector,
        vector,
        matrix,
        vector,
        vector,
        vector,
        vector,
        vector,
        vector,
        matrix,
        vector,
        matrix,
        vector,
        vector,
    )
    out_specs = (
        tokens,
        P(),
        tokens,
        matrix,
        vector,
        vector,
        matrix,
        vector,
        vector,
        vector,
        vector,
        vector,
        vector,
        matrix,
        vector,
        matrix,
        vector,
        vector,
    )
    return jax.shard_map(
        make_step(mesh.shape["shard"], mesh.shape["seq"]),
        mesh=mesh,
        in_specs=in_specs,
        out_specs=out_specs,
        check_vma=False,
    )
```
